256 devices in a mesh: dom: 64 (over y, z, core), mat: 4 (over x).
Axes of the slice: x: 4, y: 4, z: 8, core: 2. Of those that a mesh axis runs over, the one named last changes fastest.
Arguments:
- orbitals: bfloat16 [16384, 12, 32, 128], P('dom', None, 'mat')
- potential: float32 [256, 32, 128], P('dom', 'mat'), may hold values from -3 to 3
- centre_first: int32 [16384], P('dom'), may hold values from 0 to 3
- centre_second: int32 [16384], P('dom'), may hold values from 0 to 31
- centre_third: int32 [16384], P('dom'), may hold values from 0 to 127
- correlation_pairs: int32 [128, 5, 2], P('dom'), may hold values from 0 to 1, as said below
Outputs:
- gram_rows: float32 [5, 256, 16384], P(None, 'mat', 'dom')
- hamiltonian_rows: float32 [5, 256, 16384], P(None, 'mat', 'dom')
The draws below stay inside these ranges and needn't reach their ends.
Inputs may be any that keep to these rules, and one draw needn't show every extreme that they name: correlation_pairs[g, k, b] refers to block b of the domain k - 2 away from block g's owner (wrapping); the pattern is symmetric between the two blocks, and every pair of blocks of one domain is 1.
All inputs are finite; a program needn't handle non-finite values.
Results may differ from the reference program's by a relative error of at most 0.00043.
Values may be sent and summed in bfloat16 or wider, within the bound.
A program may use at most 128 MiB of HBM per device.

```python
import math
import jax
import jax.numpy as jnp
from jax import lax

ORB = 128
BLK_DEV = 2
CX = 4
CZ = 128
RAD = 6
NBLK = 128
ORBS = 16384
NX = 256
NY = 32
N_DOM = 64


def draw_orbitals(key, part):
    noise_key, shared_key = jax.random.split(key, 2)
    full_shape = (ORBS, 3 * CX, NY, CZ)
    rough_part = jax.random.normal(noise_key, full_shape, jnp.float32)
    shared = jax.random.normal(shared_key, (NBLK, 1, 3 * CX, NY, CZ), jnp.float32)
    shared = jnp.broadcast_to(shared, (NBLK, ORB, 3 * CX, NY, CZ)).reshape(full_shape)
    return (2.0 * (rough_part + 0.3 * shared) / math.sqrt(4.0 * RAD ** 3)).astype(jnp.bfloat16)


def draw_correlation_pairs(key, part):
    votes = jax.random.randint(key, (NBLK, 5, BLK_DEV), 0, 4)
    blocks = jnp.arange(NBLK, dtype=jnp.int32)
    owners = blocks // BLK_DEV
    member = blocks % BLK_DEV
    reach = jnp.arange(5, dtype=jnp.int32)
    column = jnp.arange(BLK_DEV, dtype=jnp.int32)
    domains = NBLK // BLK_DEV
    partner = jnp.mod(owners[:, None, None] + reach[None, :, None] - 2, domains) * BLK_DEV + column[None, None, :]
    mirror = votes[partner, (4 - reach)[None, :, None], member[:, None, None]]
    strongest = jnp.maximum(votes, mirror)
    needed = jnp.array([3, 2, 0, 2, 3], dtype=jnp.int32)[None, :, None]
    return (strongest >= needed).astype(jnp.int32)


def plant(values, key, low, top_value):
    place = [jax.random.randint(jax.random.fold_in(key, axis), (), 0, length) for axis, length in enumerate(values.shape)]
    widest = values.shape.index(max(values.shape))
    neighbour = place[:widest] + [(place[widest] + 1) % values.shape[widest]] + place[widest + 1:]
    return values.at[tuple(place)].set(low).at[tuple(neighbour)].set(top_value)


def steps_of(own_key, extent, shards, low, high):
    loudness = 1.0
    for position, parts in shards:
        heights = jax.random.uniform(jax.random.fold_in(jax.random.fold_in(own_key, 6), position), (parts,), jnp.float32, low / len(shards), high / len(shards))
        loudness = loudness * jnp.repeat(jnp.exp(heights), extent[position] // parts).reshape((-1,) + (1,) * (len(extent) - 1 - position))
    return loudness


def setup_inputs(seed: int = 0) -> dict:
    key_list = jax.random.split(jax.random.key(seed), 7)
    return {
        "orbitals": draw_orbitals(jax.random.fold_in(key_list[6], 71), 0),
        "potential": jnp.clip(jax.random.uniform(key_list[1], (NX, NY, CZ), jnp.float32, -3.0, 3.0) * steps_of(key_list[1], (NX, NY, CZ), ((0, 64), (1, 4)), -0.4, 0.0), -3.0, 3.0),
        "centre_first": plant(jax.random.randint(key_list[2], (ORBS,), 0, CX), jax.random.fold_in(key_list[2], 1), 0, CX - 1).astype(jnp.int32),
        "centre_second": plant(jax.random.randint(key_list[3], (ORBS,), 0, NY), jax.random.fold_in(key_list[3], 1), 0, NY - 1).astype(jnp.int32),
        "centre_third": plant(jax.random.randint(key_list[4], (ORBS,), 0, CZ), jax.random.fold_in(key_list[4], 1), 0, CZ - 1).astype(jnp.int32),
        "correlation_pairs": draw_correlation_pairs(jax.random.fold_in(key_list[6], 71), 0),
    }


def sphere_mask(centre_first, centre_second, centre_third, window_cells, patch_cells, second_cells, second_start, second_total, third_cells):
    planes = lax.iota(jnp.int32, window_cells)
    off_first = planes[None, :] - (patch_cells + centre_first[:, None])
    interior = (planes >= 1) & (planes <= window_cells - 2)
    second_coord = second_start + lax.iota(jnp.int32, second_cells)
    off_second = jnp.mod(second_coord[None, :] - centre_second[:, None], second_total)
    off_second = jnp.minimum(off_second, second_total - off_second)
    off_third = lax.iota(jnp.int32, third_cells)[None, :] - centre_third[:, None]
    radius = window_cells // 2
    distance = (off_first * off_first)[:, :, None, None] + (off_second * off_second)[:, None, :, None] + (off_third * off_third)[:, None, None, :]
    return (distance <= radius * radius) & interior[None, :, None, None]


def stencil(extended, potential_slab):
    centre_cells = extended[:, 1:-1, 1:-1, :].astype(jnp.float32)
    beside = extended[:, 2:, 1:-1, :].astype(jnp.float32) + extended[:, :-2, 1:-1, :].astype(jnp.float32)
    beside = beside + extended[:, 1:-1, 2:, :].astype(jnp.float32) + extended[:, 1:-1, :-2, :].astype(jnp.float32)
    third_padded = jnp.pad(centre_cells, ((0, 0), (0, 0), (0, 0), (1, 1)))
    beside = beside + third_padded[..., 2:] + third_padded[..., :-2]
    return 0.5 * (6.0 * centre_cells - beside) + potential_slab[None] * centre_cells


def reference(orbitals, potential, centre_first, centre_second, centre_third, correlation_pairs):
    block_orbs = BLK_DEV * ORB
    wrapped_potential = jnp.concatenate([potential[NX - CX:], potential, potential[:CX]], axis=0)

    def window_fields(owner_index):
        first_row = owner_index * block_orbs
        values = lax.dynamic_slice_in_dim(orbitals, first_row, block_orbs, 0)
        firsts = lax.dynamic_slice_in_dim(centre_first, first_row, block_orbs, 0)
        seconds = lax.dynamic_slice_in_dim(centre_second, first_row, block_orbs, 0)
        thirds = lax.dynamic_slice_in_dim(centre_third, first_row, block_orbs, 0)
        inside = sphere_mask(firsts, seconds, thirds, 3 * CX, CX, NY, 0, NY, CZ)
        masked = jnp.where(inside, values, jnp.zeros_like(values))
        padded = jnp.pad(masked, ((0, 0), (0, 0), (1, 1), (0, 0)), mode="wrap")
        padded = jnp.pad(padded, ((0, 0), (1, 1), (0, 0), (0, 0)))
        potential_window = lax.dynamic_slice_in_dim(wrapped_potential, owner_index * CX, 3 * CX, 0)
        applied = stencil(padded, potential_window).astype(jnp.bfloat16)
        return masked, applied

    def domain_terms(domain):
        orbital_parts = []
        applied_parts = []
        for slot_index in range(3):
            owner_index = jnp.mod(domain - 1 + slot_index, N_DOM).astype(jnp.int32)
            masked, applied = window_fields(owner_index)
            low_plane = (2 - slot_index) * CX
            orbital_parts.append(masked[:, low_plane:low_plane + CX])
            applied_parts.append(applied[:, low_plane:low_plane + CX])
        orbital_block = jnp.concatenate(orbital_parts, 0).reshape(3 * block_orbs, -1)
        applied_block = jnp.concatenate(applied_parts, 0).reshape(3 * block_orbs, -1)
        gram_full = lax.dot_general(orbital_block, orbital_block, (((1,), (1,)), ((), ())), preferred_element_type=jnp.float32)
        energy_full = lax.dot_general(applied_block, orbital_block, (((1,), (1,)), ((), ())), preferred_element_type=jnp.float32)
        return gram_full, energy_full

    gram_terms, energy_terms = lax.map(domain_terms, jnp.arange(N_DOM, dtype=jnp.int32))

    def assemble(partials):
        shaped = partials.reshape(N_DOM, 3, block_orbs, 3, block_orbs)
        assembled = jnp.zeros((N_DOM, 5, block_orbs, block_orbs), jnp.float32)
        for slot_index in range(3):
            strip_part = jnp.roll(shaped[:, :, :, slot_index, :], slot_index - 1, axis=0)
            assembled = assembled + jnp.pad(strip_part, ((0, 0), (2 - slot_index, slot_index), (0, 0), (0, 0)))
        return jnp.transpose(assembled, (1, 2, 0, 3)).reshape(5, block_orbs, ORBS)

    weights = correlation_pairs.astype(jnp.float32)
    column_weights = jnp.repeat(weights, ORB, axis=2)
    full_weights = jnp.repeat(column_weights, ORB, axis=0)
    select = jnp.transpose(full_weights, (1, 2, 0))
    return assemble(gram_terms) * select, assemble(energy_terms) * select
```

```python
import jax
import jax.numpy as jnp
from jax import lax
from jax.sharding import PartitionSpec as P


def extended_2(array, sides, width):
    for axis, dim in sides:
        size, length = (lax.axis_size(axis), array.shape[dim])
        up = [(i, (i + 1) % size) for i in range(size)]
        down = [(j, i) for i, j in up]
        last = lax.slice_in_dim(array, length - width, length, axis=dim)
        first = lax.slice_in_dim(array, 0, width, axis=dim)
        before = lax.ppermute(last, axis, up)
        after = lax.ppermute(first, axis, down)
        array = jnp.concatenate([before, array, after], axis=dim)
    return array


def passed_along(block, axis, distance):
    devices = range(lax.axis_size(axis))
    route = [((i - distance) % len(devices), i) for i in devices]
    return lax.ppermute(block, axis, route)


def sphere_mask(
    centre_first,
    centre_second,
    centre_third,
    window_cells,
    patch_cells,
    second_cells,
    second_start,
    second_total,
    third_cells,
):
    planes = lax.iota(jnp.int32, window_cells)
    off_first = planes[None, :] - (patch_cells + centre_first[:, None])
    interior = (planes >= 1) & (planes <= window_cells - 2)
    second_coord = second_start + lax.iota(jnp.int32, second_cells)
    off_second = jnp.mod(second_coord[None, :] - centre_second[:, None], second_total)
    off_second = jnp.minimum(off_second, second_total - off_second)
    off_third = lax.iota(jnp.int32, third_cells)[None, :] - centre_third[:, None]
    radius = window_cells // 2
    distance = (
        (off_first * off_first)[:, :, None, None]
        + (off_second * off_second)[:, None, :, None]
        + (off_third * off_third)[:, None, None, :]
    )
    return (distance <= radius * radius) & interior[None, :, None, None]


def stencil(extended, potential_slab):
    centre_cells = extended[:, 1:-1, 1:-1, :].astype(jnp.float32)
    beside = extended[:, 2:, 1:-1, :].astype(jnp.float32) + extended[:, :-2, 1:-1, :].astype(
        jnp.float32
    )
    beside = (
        beside
        + extended[:, 1:-1, 2:, :].astype(jnp.float32)
        + extended[:, 1:-1, :-2, :].astype(jnp.float32)
    )
    third_padded = jnp.pad(centre_cells, ((0, 0), (0, 0), (0, 0), (1, 1)))
    beside = beside + third_padded[..., 2:] + third_padded[..., :-2]
    return 0.5 * (6.0 * centre_cells - beside) + potential_slab[None] * centre_cells


def pair_product(left, right):
    return lax.dot_general(
        left, right, (((1, 2, 3), (1, 2, 3)), ((), ())), preferred_element_type=jnp.float32
    )


def on_device(orbitals, potential, centre_first, centre_second, centre_third, correlation_pairs):
    block_orbs, window_cells, second_cells, third_cells = orbitals.shape
    patch_cells = potential.shape[0]
    local_blocks = correlation_pairs.shape[0]
    per_block = block_orbs // local_blocks
    mat_count = lax.axis_size("mat")
    second_start = lax.axis_index("mat") * second_cells
    inside = sphere_mask(
        centre_first,
        centre_second,
        centre_third,
        window_cells,
        patch_cells,
        second_cells,
        second_start,
        second_cells * mat_count,
        third_cells,
    )
    masked = jnp.where(inside, orbitals, jnp.zeros_like(orbitals))
    upper_start = 2 * patch_cells
    phi_slots = [
        passed_along(masked[:, upper_start:], "dom", 1),
        masked[:, patch_cells:upper_start],
        passed_along(masked[:, :patch_cells], "dom", -1),
    ]
    rimmed = extended_2(masked, (("mat", 2),), 1)
    rimmed = jnp.pad(rimmed, ((0, 0), (1, 1), (0, 0), (0, 0)))
    potential_window = extended_2(potential, (("dom", 0),), patch_cells)
    applied = stencil(rimmed, potential_window).astype(jnp.bfloat16)
    applied_slots = [
        passed_along(applied[:, upper_start:], "dom", 1),
        applied[:, patch_cells:upper_start],
        passed_along(applied[:, :patch_cells], "dom", -1),
    ]
    gram_full = jnp.stack(
        [jnp.stack([pair_product(phi_slots[a], phi_slots[b]) for b in range(3)], 1) for a in range(3)]
    )
    energy_full = jnp.stack(
        [
            jnp.stack([pair_product(applied_slots[a], phi_slots[b]) for b in range(3)], 1)
            for a in range(3)
        ]
    )
    gram_part = lax.psum_scatter(gram_full, "mat", scatter_dimension=1, tiled=True)
    energy_part = lax.psum_scatter(energy_full, "mat", scatter_dimension=1, tiled=True)
    col_count = block_orbs // mat_count
    strips = jnp.stack([gram_part, energy_part])
    assembled = jnp.pad(strips[:, :, :, 1], ((0, 0), (1, 1), (0, 0), (0, 0)))
    for slot_index, offset in ((0, -1), (2, 1)):
        arrived = passed_along(strips[:, :, :, slot_index], "dom", offset)
        assembled = assembled + jnp.pad(
            arrived, ((0, 0), (2 - slot_index, slot_index), (0, 0), (0, 0))
        )
    columns = lax.axis_index("mat") * col_count + lax.iota(jnp.int32, col_count)
    block_ids = lax.iota(jnp.int32, local_blocks)
    column_pick = ((columns // per_block)[:, None] == block_ids[None, :]).astype(jnp.float32)
    row_pick = (
        (lax.iota(jnp.int32, block_orbs) // per_block)[:, None] == block_ids[None, :]
    ).astype(jnp.float32)
    select = jnp.einsum(
        "rkb,cb,ar->kca", correlation_pairs.astype(jnp.float32), column_pick, row_pick
    )
    return (assembled[0] * select, assembled[1] * select)


def solution(mesh):
    return jax.shard_map(
        on_device,
        mesh=mesh,
        in_specs=(
            P("dom", None, "mat", None),
            P("dom", "mat", None),
            P("dom"),
            P("dom"),
            P("dom"),
            P("dom", None, None),
        ),
        out_specs=(P(None, "mat", "dom"), P(None, "mat", "dom")),
        check_vma=False,
    )
```

```python
import jax
import jax.numpy as jnp
from jax import lax
from jax.sharding import PartitionSpec as P


def extended_2(array, sides, width):
    for axis, dim in sides:
        size, length = (lax.axis_size(axis), array.shape[dim])
        up = [(i, (i + 1) % size) for i in range(size)]
        down = [(j, i) for i, j in up]
        last = lax.slice_in_dim(array, length - width, length, axis=dim)
        first = lax.slice_in_dim(array, 0, width, axis=dim)
        before = lax.ppermute(last, axis, up)
        after = lax.ppermute(first, axis, down)
        array = jnp.concatenate([before, array, after], axis=dim)
    return array


def passed_along(block, axis, distance):
    devices = range(lax.axis_size(axis))
    route = [((i - distance) % len(devices), i) for i in devices]
    return lax.ppermute(block, axis, route)


def sphere_mask(
    centre_first,
    centre_second,
    centre_third,
    window_cells,
    patch_cells,
    second_cells,
    second_start,
    second_total,
    third_cells,
):
    planes = lax.iota(jnp.int32, window_cells)
    off_first = planes[None, :] - (patch_cells + centre_first[:, None])
    interior = (planes >= 1) & (planes <= window_cells - 2)
    second_coord = second_start + lax.iota(jnp.int32, second_cells)
    off_second = jnp.mod(second_coord[None, :] - centre_second[:, None], second_total)
    off_second = jnp.minimum(off_second, second_total - off_second)
    off_third = lax.iota(jnp.int32, third_cells)[None, :] - centre_third[:, None]
    radius = window_cells // 2
    distance = (
        (off_first * off_first)[:, :, None, None]
        + (off_second * off_second)[:, None, :, None]
        + (off_third * off_third)[:, None, None, :]
    )
    return (distance <= radius * radius) & interior[None, :, None, None]


def stencil(extended, potential_slab):
    centre_cells = extended[:, 1:-1, 1:-1, :].astype(jnp.float32)
    beside = extended[:, 2:, 1:-1, :].astype(jnp.float32) + extended[:, :-2, 1:-1, :].astype(
        jnp.float32
    )
    beside = (
        beside
        + extended[:, 1:-1, 2:, :].astype(jnp.float32)
        + extended[:, 1:-1, :-2, :].astype(jnp.float32)
    )
    third_padded = jnp.pad(centre_cells, ((0, 0), (0, 0), (0, 0), (1, 1)))
    beside = beside + third_padded[..., 2:] + third_padded[..., :-2]
    return 0.5 * (6.0 * centre_cells - beside) + potential_slab[None] * centre_cells


def pair_product(left, right):
    return lax.dot_general(
        left, right, (((1, 2, 3), (1, 2, 3)), ((), ())), preferred_element_type=jnp.float32
    )


def on_device(orbitals, potential, centre_first, centre_second, centre_third, correlation_pairs):
    block_orbs, window_cells, second_cells, third_cells = orbitals.shape
    patch_cells = potential.shape[0]
    local_blocks = correlation_pairs.shape[0]
    per_block = block_orbs // local_blocks
    mat_count = lax.axis_size("mat")
    second_start = lax.axis_index("mat") * second_cells
    inside = sphere_mask(
        centre_first,
        centre_second,
        centre_third,
        window_cells,
        patch_cells,
        second_cells,
        second_start,
        second_cells * mat_count,
        third_cells,
    )
    masked = jnp.where(inside, orbitals, jnp.zeros_like(orbitals))
    upper_start = 2 * patch_cells
    to_right = masked[:, upper_start - 1 : window_cells - 1]
    to_left = masked[:, 1 : patch_cells + 1]
    from_left = passed_along(to_right, "dom", 1)
    from_right = passed_along(to_left, "dom", -1)
    mat_size = lax.axis_size("mat")
    up = [(i, (i + 1) % mat_size) for i in range(mat_size)]
    down = [(j, i) for i, j in up]
    row_above = lax.ppermute(masked[:, :, second_cells - 1], "mat", up)
    row_below = lax.ppermute(masked[:, :, 0], "mat", down)
    rows_right = jnp.stack(
        [row_above[:, upper_start - 1 : window_cells - 1], row_below[:, upper_start - 1 : window_cells - 1]]
    )
    rows_left = jnp.stack([row_above[:, 1 : patch_cells + 1], row_below[:, 1 : patch_cells + 1]])
    rows_from_left = passed_along(rows_right, "dom", 1)
    rows_from_right = passed_along(rows_left, "dom", -1)

    def with_rows(planes, rows):
        return jnp.concatenate([rows[0][:, :, None], planes, rows[1][:, :, None]], axis=2)

    zero_plane = jnp.zeros_like(masked[:, :1])
    zero_rows = jnp.zeros((2, block_orbs, 1, third_cells), masked.dtype)
    own_ext = with_rows(
        masked[:, patch_cells - 1 : upper_start + 1],
        jnp.stack([row_above[:, patch_cells - 1 : upper_start + 1], row_below[:, patch_cells - 1 : upper_start + 1]]),
    )
    left_ext = with_rows(
        jnp.concatenate([from_left, zero_plane, zero_plane], axis=1),
        jnp.concatenate([rows_from_left, zero_rows, zero_rows], axis=2),
    )
    right_ext = with_rows(
        jnp.concatenate([zero_plane, zero_plane, from_right], axis=1),
        jnp.concatenate([zero_rows, zero_rows, rows_from_right], axis=2),
    )
    phi_slots = [
        jnp.concatenate([from_left[:, 1:], zero_plane], axis=1),
        masked[:, patch_cells:upper_start],
        jnp.concatenate([zero_plane, from_right[:, :-1]], axis=1),
    ]
    applied_slots = [
        stencil(ext, potential).astype(jnp.bfloat16) for ext in (left_ext, own_ext, right_ext)
    ]
    gram_full = jnp.stack(
        [jnp.stack([pair_product(phi_slots[a], phi_slots[b]) for b in range(3)], 1) for a in range(3)]
    )
    energy_full = jnp.stack(
        [
            jnp.stack([pair_product(applied_slots[a], phi_slots[b]) for b in range(3)], 1)
            for a in range(3)
        ]
    )
    gram_part = lax.psum_scatter(gram_full, "mat", scatter_dimension=1, tiled=True)
    energy_part = lax.psum_scatter(energy_full, "mat", scatter_dimension=1, tiled=True)
    col_count = block_orbs // mat_count
    strips = jnp.stack([gram_part, energy_part])
    assembled = jnp.pad(strips[:, :, :, 1], ((0, 0), (1, 1), (0, 0), (0, 0)))
    for slot_index, offset in ((0, -1), (2, 1)):
        arrived = passed_along(strips[:, :, :, slot_index], "dom", offset)
        assembled = assembled + jnp.pad(
            arrived, ((0, 0), (2 - slot_index, slot_index), (0, 0), (0, 0))
        )
    columns = lax.axis_index("mat") * col_count + lax.iota(jnp.int32, col_count)
    block_ids = lax.iota(jnp.int32, local_blocks)
    column_pick = ((columns // per_block)[:, None] == block_ids[None, :]).astype(jnp.float32)
    row_pick = (
        (lax.iota(jnp.int32, block_orbs) // per_block)[:, None] == block_ids[None, :]
    ).astype(jnp.float32)
    select = jnp.einsum(
        "rkb,cb,ar->kca", correlation_pairs.astype(jnp.float32), column_pick, row_pick
    )
    return (assembled[0] * select, assembled[1] * select)


def solution(mesh):
    return jax.shard_map(
        on_device,
        mesh=mesh,
        in_specs=(
            P("dom", None, "mat", None),
            P("dom", "mat", None),
            P("dom"),
            P("dom"),
            P("dom"),
            P("dom", None, None),
        ),
        out_specs=(P(None, "mat", "dom"), P(None, "mat", "dom")),
        check_vma=False,
    )
```

```python
import jax
import jax.numpy as jnp
from jax import lax
from jax.sharding import PartitionSpec as P


def extended_2(array, sides, width):
    for axis, dim in sides:
        size, length = (lax.axis_size(axis), array.shape[dim])
        up = [(i, (i + 1) % size) for i in range(size)]
        down = [(j, i) for i, j in up]
        last = lax.slice_in_dim(array, length - width, length, axis=dim)
        first = lax.slice_in_dim(array, 0, width, axis=dim)
        before = lax.ppermute(last, axis, up)
        after = lax.ppermute(first, axis, down)
        array = jnp.concatenate([before, array, after], axis=dim)
    return array


def passed_along(block, axis, distance):
    devices = range(lax.axis_size(axis))
    route = [((i - distance) % len(devices), i) for i in devices]
    return lax.ppermute(block, axis, route)


def sphere_mask(
    centre_first,
    centre_second,
    centre_third,
    window_cells,
    patch_cells,
    second_cells,
    second_start,
    second_total,
    third_cells,
):
    planes = lax.iota(jnp.int32, window_cells)
    off_first = planes[None, :] - (patch_cells + centre_first[:, None])
    interior = (planes >= 1) & (planes <= window_cells - 2)
    second_coord = second_start + lax.iota(jnp.int32, second_cells)
    off_second = jnp.mod(second_coord[None, :] - centre_second[:, None], second_total)
    off_second = jnp.minimum(off_second, second_total - off_second)
    off_third = lax.iota(jnp.int32, third_cells)[None, :] - centre_third[:, None]
    radius = window_cells // 2
    distance = (
        (off_first * off_first)[:, :, None, None]
        + (off_second * off_second)[:, None, :, None]
        + (off_third * off_third)[:, None, None, :]
    )
    return (distance <= radius * radius) & interior[None, :, None, None]


def stencil(extended, potential_slab):
    centre_cells = extended[:, 1:-1, 1:-1, :].astype(jnp.float32)
    beside = extended[:, 2:, 1:-1, :].astype(jnp.float32) + extended[:, :-2, 1:-1, :].astype(
        jnp.float32
    )
    beside = (
        beside
        + extended[:, 1:-1, 2:, :].astype(jnp.float32)
        + extended[:, 1:-1, :-2, :].astype(jnp.float32)
    )
    third_padded = jnp.pad(centre_cells, ((0, 0), (0, 0), (0, 0), (1, 1)))
    beside = beside + third_padded[..., 2:] + third_padded[..., :-2]
    return 0.5 * (6.0 * centre_cells - beside) + potential_slab[None] * centre_cells


def pair_product(left, right):
    return lax.dot_general(
        left, right, (((1, 2, 3), (1, 2, 3)), ((), ())), preferred_element_type=jnp.float32
    )


def ring_scatter(full):
    count = lax.axis_size("mat")
    me = lax.axis_index("mat")
    share = full.shape[1] // count
    split = full.shape[-1] // 2
    halves = (full[..., :split], full[..., split:])
    forward = [(i, (i + 1) % count) for i in range(count)]
    backward = [((i + 1) % count, i) for i in range(count)]

    def chunk(values, index):
        return lax.dynamic_slice_in_dim(values, index * share, share, axis=1)

    ahead = chunk(halves[0], lax.rem(me + count - 1, count))
    behind = chunk(halves[1], lax.rem(me + 1, count))
    for step in range(count - 1):
        ahead = lax.ppermute(ahead, "mat", forward)
        behind = lax.ppermute(behind, "mat", backward)
        ahead = ahead + chunk(halves[0], lax.rem(me + 2 * count - 2 - step, count))
        behind = behind + chunk(halves[1], lax.rem(me + 2 + step, count))
    return jnp.concatenate([ahead, behind], axis=-1)


def on_device(orbitals, potential, centre_first, centre_second, centre_third, correlation_pairs):
    block_orbs, window_cells, second_cells, third_cells = orbitals.shape
    patch_cells = potential.shape[0]
    local_blocks = correlation_pairs.shape[0]
    per_block = block_orbs // local_blocks
    mat_count = lax.axis_size("mat")
    second_start = lax.axis_index("mat") * second_cells
    inside = sphere_mask(
        centre_first,
        centre_second,
        centre_third,
        window_cells,
        patch_cells,
        second_cells,
        second_start,
        second_cells * mat_count,
        third_cells,
    )
    masked = jnp.where(inside, orbitals, jnp.zeros_like(orbitals))
    upper_start = 2 * patch_cells
    to_right = masked[:, upper_start - 1 : window_cells - 1]
    to_left = masked[:, 1 : patch_cells + 1]
    from_left = passed_along(to_right, "dom", 1)
    from_right = passed_along(to_left, "dom", -1)
    mat_size = lax.axis_size("mat")
    up = [(i, (i + 1) % mat_size) for i in range(mat_size)]
    down = [(j, i) for i, j in up]
    row_above = lax.ppermute(masked[:, :, second_cells - 1], "mat", up)
    row_below = lax.ppermute(masked[:, :, 0], "mat", down)
    rows_right = jnp.stack(
        [row_above[:, upper_start - 1 : window_cells - 1], row_below[:, upper_start - 1 : window_cells - 1]]
    )
    rows_left = jnp.stack([row_above[:, 1 : patch_cells + 1], row_below[:, 1 : patch_cells + 1]])
    rows_from_left = passed_along(rows_right, "dom", 1)
    rows_from_right = passed_along(rows_left, "dom", -1)

    def with_rows(planes, rows):
        return jnp.concatenate([rows[0][:, :, None], planes, rows[1][:, :, None]], axis=2)

    zero_plane = jnp.zeros_like(masked[:, :1])
    zero_rows = jnp.zeros((2, block_orbs, 1, third_cells), masked.dtype)
    own_ext = with_rows(
        masked[:, patch_cells - 1 : upper_start + 1],
        jnp.stack([row_above[:, patch_cells - 1 : upper_start + 1], row_below[:, patch_cells - 1 : upper_start + 1]]),
    )
    left_ext = with_rows(
        jnp.concatenate([from_left, zero_plane, zero_plane], axis=1),
        jnp.concatenate([rows_from_left, zero_rows, zero_rows], axis=2),
    )
    right_ext = with_rows(
        jnp.concatenate([zero_plane, zero_plane, from_right], axis=1),
        jnp.concatenate([zero_rows, zero_rows, rows_from_right], axis=2),
    )
    phi_slots = [
        jnp.concatenate([from_left[:, 1:], zero_plane], axis=1),
        masked[:, patch_cells:upper_start],
        jnp.concatenate([zero_plane, from_right[:, :-1]], axis=1),
    ]
    applied_slots = [
        stencil(ext, potential).astype(jnp.bfloat16) for ext in (left_ext, own_ext, right_ext)
    ]
    gram_full = jnp.stack(
        [jnp.stack([pair_product(phi_slots[a], phi_slots[b]) for b in range(3)], 1) for a in range(3)]
    )
    energy_full = jnp.stack(
        [
            jnp.stack([pair_product(applied_slots[a], phi_slots[b]) for b in range(3)], 1)
            for a in range(3)
        ]
    )
    gram_part = ring_scatter(gram_full)
    energy_part = ring_scatter(energy_full)
    col_count = block_orbs // mat_count
    strips = jnp.stack([gram_part, energy_part])
    assembled = jnp.pad(strips[:, :, :, 1], ((0, 0), (1, 1), (0, 0), (0, 0)))
    for slot_index, offset in ((0, -1), (2, 1)):
        arrived = passed_along(strips[:, :, :, slot_index], "dom", offset)
        assembled = assembled + jnp.pad(
            arrived, ((0, 0), (2 - slot_index, slot_index), (0, 0), (0, 0))
        )
    columns = lax.axis_index("mat") * col_count + lax.iota(jnp.int32, col_count)
    block_ids = lax.iota(jnp.int32, local_blocks)
    column_pick = ((columns // per_block)[:, None] == block_ids[None, :]).astype(jnp.float32)
    row_pick = (
        (lax.iota(jnp.int32, block_orbs) // per_block)[:, None] == block_ids[None, :]
    ).astype(jnp.float32)
    select = jnp.einsum(
        "rkb,cb,ar->kca", correlation_pairs.astype(jnp.float32), column_pick, row_pick
    )
    return (assembled[0] * select, assembled[1] * select)


def solution(mesh):
    return jax.shard_map(
        on_device,
        mesh=mesh,
        in_specs=(
            P("dom", None, "mat", None),
            P("dom", "mat", None),
            P("dom"),
            P("dom"),
            P("dom"),
            P("dom", None, None),
        ),
        out_specs=(P(None, "mat", "dom"), P(None, "mat", "dom")),
        check_vma=False,
    )
```

```python
import jax
import jax.numpy as jnp
from jax import lax
from jax.sharding import PartitionSpec as P


def extended_2(array, sides, width):
    for axis, dim in sides:
        size, length = (lax.axis_size(axis), array.shape[dim])
        up = [(i, (i + 1) % size) for i in range(size)]
        down = [(j, i) for i, j in up]
        last = lax.slice_in_dim(array, length - width, length, axis=dim)
        first = lax.slice_in_dim(array, 0, width, axis=dim)
        before = lax.ppermute(last, axis, up)
        after = lax.ppermute(first, axis, down)
        array = jnp.concatenate([before, array, after], axis=dim)
    return array


def passed_along(block, axis, distance):
    devices = range(lax.axis_size(axis))
    route = [((i - distance) % len(devices), i) for i in devices]
    return lax.ppermute(block, axis, route)


def sphere_mask(
    centre_first,
    centre_second,
    centre_third,
    window_cells,
    patch_cells,
    second_cells,
    second_start,
    second_total,
    third_cells,
):
    planes = lax.iota(jnp.int32, window_cells)
    off_first = planes[None, :] - (patch_cells + centre_first[:, None])
    interior = (planes >= 1) & (planes <= window_cells - 2)
    second_coord = second_start + lax.iota(jnp.int32, second_cells)
    off_second = jnp.mod(second_coord[None, :] - centre_second[:, None], second_total)
    off_second = jnp.minimum(off_second, second_total - off_second)
    off_third = lax.iota(jnp.int32, third_cells)[None, :] - centre_third[:, None]
    radius = window_cells // 2
    distance = (
        (off_first * off_first)[:, :, None, None]
        + (off_second * off_second)[:, None, :, None]
        + (off_third * off_third)[:, None, None, :]
    )
    return (distance <= radius * radius) & interior[None, :, None, None]


def stencil(extended, potential_slab):
    centre_cells = extended[:, 1:-1, 1:-1, :].astype(jnp.float32)
    beside = extended[:, 2:, 1:-1, :].astype(jnp.float32) + extended[:, :-2, 1:-1, :].astype(
        jnp.float32
    )
    beside = (
        beside
        + extended[:, 1:-1, 2:, :].astype(jnp.float32)
        + extended[:, 1:-1, :-2, :].astype(jnp.float32)
    )
    third_padded = jnp.pad(centre_cells, ((0, 0), (0, 0), (0, 0), (1, 1)))
    beside = beside + third_padded[..., 2:] + third_padded[..., :-2]
    return 0.5 * (6.0 * centre_cells - beside) + potential_slab[None] * centre_cells


def pair_product(left, right):
    return lax.dot_general(
        left, right, (((1, 2, 3), (1, 2, 3)), ((), ())), preferred_element_type=jnp.float32
    )


def ring_scatter(full):
    count = lax.axis_size("mat")
    me = lax.axis_index("mat")
    share = full.shape[1] // count
    split = full.shape[-1] // 2
    halves = (full[..., :split], full[..., split:])
    forward = [(i, (i + 1) % count) for i in range(count)]
    backward = [((i + 1) % count, i) for i in range(count)]

    def chunk(values, index):
        return lax.dynamic_slice_in_dim(values, index * share, share, axis=1)

    ahead = chunk(halves[0], lax.rem(me + count - 1, count))
    behind = chunk(halves[1], lax.rem(me + 1, count))
    for step in range(count - 1):
        ahead = lax.ppermute(ahead, "mat", forward)
        behind = lax.ppermute(behind, "mat", backward)
        ahead = ahead + chunk(halves[0], lax.rem(me + 2 * count - 2 - step, count))
        behind = behind + chunk(halves[1], lax.rem(me + 2 + step, count))
    return jnp.concatenate([ahead, behind], axis=-1)


def on_device(orbitals, potential, centre_first, centre_second, centre_third, correlation_pairs):
    block_orbs, window_cells, second_cells, third_cells = orbitals.shape
    patch_cells = potential.shape[0]
    local_blocks = correlation_pairs.shape[0]
    per_block = block_orbs // local_blocks
    mat_count = lax.axis_size("mat")
    second_start = lax.axis_index("mat") * second_cells
    inside = sphere_mask(
        centre_first,
        centre_second,
        centre_third,
        window_cells,
        patch_cells,
        second_cells,
        second_start,
        second_cells * mat_count,
        third_cells,
    )
    masked = jnp.where(inside, orbitals, jnp.zeros_like(orbitals))
    upper_start = 2 * patch_cells
    to_right = masked[:, upper_start - 1 : window_cells - 1]
    to_left = masked[:, 1 : patch_cells + 1]
    from_left = passed_along(to_right, "dom", 1)
    from_right = passed_along(to_left, "dom", -1)
    mat_size = lax.axis_size("mat")
    up = [(i, (i + 1) % mat_size) for i in range(mat_size)]
    down = [(j, i) for i, j in up]
    row_above = lax.ppermute(masked[:, :, second_cells - 1], "mat", up)
    row_below = lax.ppermute(masked[:, :, 0], "mat", down)
    rows_right = jnp.stack(
        [row_above[:, upper_start - 1 : window_cells - 1], row_below[:, upper_start - 1 : window_cells - 1]]
    )
    rows_left = jnp.stack([row_above[:, 1 : patch_cells + 1], row_below[:, 1 : patch_cells + 1]])
    rows_from_left = passed_along(rows_right, "dom", 1)
    rows_from_right = passed_along(rows_left, "dom", -1)

    def with_rows(planes, rows):
        return jnp.concatenate([rows[0][:, :, None], planes, rows[1][:, :, None]], axis=2)

    zero_plane = jnp.zeros_like(masked[:, :1])
    zero_rows = jnp.zeros((2, block_orbs, 1, third_cells), masked.dtype)
    own_ext = with_rows(
        masked[:, patch_cells - 1 : upper_start + 1],
        jnp.stack([row_above[:, patch_cells - 1 : upper_start + 1], row_below[:, patch_cells - 1 : upper_start + 1]]),
    )
    left_ext = with_rows(
        jnp.concatenate([from_left, zero_plane, zero_plane], axis=1),
        jnp.concatenate([rows_from_left, zero_rows, zero_rows], axis=2),
    )
    right_ext = with_rows(
        jnp.concatenate([zero_plane, zero_plane, from_right], axis=1),
        jnp.concatenate([zero_rows, zero_rows, rows_from_right], axis=2),
    )
    phi_slots = [
        jnp.concatenate([from_left[:, 1:], zero_plane], axis=1),
        masked[:, patch_cells:upper_start],
        jnp.concatenate([zero_plane, from_right[:, :-1]], axis=1),
    ]
    gram_full = jnp.stack(
        [jnp.stack([pair_product(phi_slots[a], phi_slots[b]) for b in range(3)], 1) for a in range(3)]
    )
    gram_full, left_ext, right_ext = lax.optimization_barrier((gram_full, left_ext, right_ext))
    gram_part = ring_scatter(gram_full)
    applied_slots = [
        stencil(ext, potential).astype(jnp.bfloat16) for ext in (left_ext, own_ext, right_ext)
    ]
    energy_full = jnp.stack(
        [
            jnp.stack([pair_product(applied_slots[a], phi_slots[b]) for b in range(3)], 1)
            for a in range(3)
        ]
    )
    energy_part = ring_scatter(energy_full)
    col_count = block_orbs // mat_count

    def row_blocks(part):
        assembled = jnp.pad(part[:, :, 1], ((1, 1), (0, 0), (0, 0)))
        for slot_index, offset in ((0, -1), (2, 1)):
            arrived = passed_along(part[:, :, slot_index], "dom", offset)
            assembled = assembled + jnp.pad(arrived, ((2 - slot_index, slot_index), (0, 0), (0, 0)))
        return assembled

    gram_rows = row_blocks(gram_part)
    energy_rows = row_blocks(energy_part)
    columns = lax.axis_index("mat") * col_count + lax.iota(jnp.int32, col_count)
    block_ids = lax.iota(jnp.int32, local_blocks)
    column_pick = ((columns // per_block)[:, None] == block_ids[None, :]).astype(jnp.float32)
    row_pick = (
        (lax.iota(jnp.int32, block_orbs) // per_block)[:, None] == block_ids[None, :]
    ).astype(jnp.float32)
    select = jnp.einsum(
        "rkb,cb,ar->kca", correlation_pairs.astype(jnp.float32), column_pick, row_pick
    )
    return (gram_rows * select, energy_rows * select)


def solution(mesh):
    return jax.shard_map(
        on_device,
        mesh=mesh,
        in_specs=(
            P("dom", None, "mat", None),
            P("dom", "mat", None),
            P("dom"),
            P("dom"),
            P("dom"),
            P("dom", None, None),
        ),
        out_specs=(P(None, "mat", "dom"), P(None, "mat", "dom")),
        check_vma=False,
    )
```

```python
import jax
import jax.numpy as jnp
from jax import lax
from jax.sharding import PartitionSpec as P


def extended_2(array, sides, width):
    for axis, dim in sides:
        size, length = (lax.axis_size(axis), array.shape[dim])
        up = [(i, (i + 1) % size) for i in range(size)]
        down = [(j, i) for i, j in up]
        last = lax.slice_in_dim(array, length - width, length, axis=dim)
        first = lax.slice_in_dim(array, 0, width, axis=dim)
        before = lax.ppermute(last, axis, up)
        after = lax.ppermute(first, axis, down)
        array = jnp.concatenate([before, array, after], axis=dim)
    return array


def passed_along(block, axis, distance):
    devices = range(lax.axis_size(axis))
    route = [((i - distance) % len(devices), i) for i in devices]
    return lax.ppermute(block, axis, route)


def sphere_mask(
    centre_first,
    centre_second,
    centre_third,
    window_cells,
    patch_cells,
    second_cells,
    second_start,
    second_total,
    third_cells,
):
    planes = lax.iota(jnp.int32, window_cells)
    off_first = planes[None, :] - (patch_cells + centre_first[:, None])
    interior = (planes >= 1) & (planes <= window_cells - 2)
    second_coord = second_start + lax.iota(jnp.int32, second_cells)
    off_second = jnp.mod(second_coord[None, :] - centre_second[:, None], second_total)
    off_second = jnp.minimum(off_second, second_total - off_second)
    off_third = lax.iota(jnp.int32, third_cells)[None, :] - centre_third[:, None]
    radius = window_cells // 2
    distance = (
        (off_first * off_first)[:, :, None, None]
        + (off_second * off_second)[:, None, :, None]
        + (off_third * off_third)[:, None, None, :]
    )
    return (distance <= radius * radius) & interior[None, :, None, None]


def stencil(extended, potential_slab):
    centre_cells = extended[:, 1:-1, 1:-1, :].astype(jnp.float32)
    beside = extended[:, 2:, 1:-1, :].astype(jnp.float32) + extended[:, :-2, 1:-1, :].astype(
        jnp.float32
    )
    beside = (
        beside
        + extended[:, 1:-1, 2:, :].astype(jnp.float32)
        + extended[:, 1:-1, :-2, :].astype(jnp.float32)
    )
    third_padded = jnp.pad(centre_cells, ((0, 0), (0, 0), (0, 0), (1, 1)))
    beside = beside + third_padded[..., 2:] + third_padded[..., :-2]
    return 0.5 * (6.0 * centre_cells - beside) + potential_slab[None] * centre_cells


def pair_product(left, right):
    return lax.dot_general(
        left, right, (((1, 2, 3), (1, 2, 3)), ((), ())), preferred_element_type=jnp.float32
    )


def ring_scatter(full, axis):
    count = lax.axis_size("mat")
    me = lax.axis_index("mat")
    share = full.shape[axis] // count
    split = full.shape[-1] // 2
    halves = (full[..., :split], full[..., split:])
    forward = [(i, (i + 1) % count) for i in range(count)]
    backward = [((i + 1) % count, i) for i in range(count)]

    def chunk(values, index):
        return lax.dynamic_slice_in_dim(values, index * share, share, axis=axis)

    ahead = chunk(halves[0], lax.rem(me + count - 1, count))
    behind = chunk(halves[1], lax.rem(me + 1, count))
    for step in range(count - 1):
        ahead = lax.ppermute(ahead, "mat", forward)
        behind = lax.ppermute(behind, "mat", backward)
        ahead = ahead + chunk(halves[0], lax.rem(me + 2 * count - 2 - step, count))
        behind = behind + chunk(halves[1], lax.rem(me + 2 + step, count))
    return jnp.concatenate([ahead, behind], axis=-1)


def on_device(orbitals, potential, centre_first, centre_second, centre_third, correlation_pairs):
    block_orbs, window_cells, second_cells, third_cells = orbitals.shape
    patch_cells = potential.shape[0]
    local_blocks = correlation_pairs.shape[0]
    per_block = block_orbs // local_blocks
    mat_count = lax.axis_size("mat")
    second_start = lax.axis_index("mat") * second_cells
    inside = sphere_mask(
        centre_first,
        centre_second,
        centre_third,
        window_cells,
        patch_cells,
        second_cells,
        second_start,
        second_cells * mat_count,
        third_cells,
    )
    masked = jnp.where(inside, orbitals, jnp.zeros_like(orbitals))
    upper_start = 2 * patch_cells
    to_right = masked[:, upper_start - 1 : window_cells - 1]
    to_left = masked[:, 1 : patch_cells + 1]
    from_left = passed_along(to_right, "dom", 1)
    from_right = passed_along(to_left, "dom", -1)
    mat_size = lax.axis_size("mat")
    up = [(i, (i + 1) % mat_size) for i in range(mat_size)]
    down = [(j, i) for i, j in up]
    row_above = lax.ppermute(masked[:, :, second_cells - 1], "mat", up)
    row_below = lax.ppermute(masked[:, :, 0], "mat", down)
    rows_right = jnp.stack(
        [row_above[:, upper_start - 1 : window_cells - 1], row_below[:, upper_start - 1 : window_cells - 1]]
    )
    rows_left = jnp.stack([row_above[:, 1 : patch_cells + 1], row_below[:, 1 : patch_cells + 1]])
    rows_from_left = passed_along(rows_right, "dom", 1)
    rows_from_right = passed_along(rows_left, "dom", -1)

    def with_rows(planes, rows):
        return jnp.concatenate([rows[0][:, :, None], planes, rows[1][:, :, None]], axis=2)

    zero_plane = jnp.zeros_like(masked[:, :1])
    zero_rows = jnp.zeros((2, block_orbs, 1, third_cells), masked.dtype)
    own_ext = with_rows(
        masked[:, patch_cells - 1 : upper_start + 1],
        jnp.stack([row_above[:, patch_cells - 1 : upper_start + 1], row_below[:, patch_cells - 1 : upper_start + 1]]),
    )
    left_ext = with_rows(
        jnp.concatenate([from_left, zero_plane, zero_plane], axis=1),
        jnp.concatenate([rows_from_left, zero_rows, zero_rows], axis=2),
    )
    right_ext = with_rows(
        jnp.concatenate([zero_plane, zero_plane, from_right], axis=1),
        jnp.concatenate([zero_rows, zero_rows, rows_from_right], axis=2),
    )
    phi_slots = [
        jnp.concatenate([from_left[:, 1:], zero_plane], axis=1),
        masked[:, patch_cells:upper_start],
        jnp.concatenate([zero_plane, from_right[:, :-1]], axis=1),
    ]
    applied_slots = [
        stencil(ext, potential).astype(jnp.bfloat16) for ext in (left_ext, own_ext, right_ext)
    ]
    gram_full = jnp.stack(
        [jnp.stack([pair_product(phi_slots[a], phi_slots[b]) for b in range(3)], 1) for a in range(3)]
    )
    energy_full = jnp.stack(
        [
            jnp.stack([pair_product(applied_slots[a], phi_slots[b]) for b in range(3)], 1)
            for a in range(3)
        ]
    )
    col_count = block_orbs // mat_count

    def row_blocks(full):
        assembled = jnp.pad(full[:, :, 1], ((1, 1), (0, 0), (0, 0)))
        for slot_index, offset in ((0, -1), (2, 1)):
            arrived = passed_along(full[:, :, slot_index], "dom", offset)
            assembled = assembled + jnp.pad(arrived, ((2 - slot_index, slot_index), (0, 0), (0, 0)))
        return assembled

    both = jnp.stack([row_blocks(gram_full), row_blocks(energy_full)])
    gram_rows, energy_rows = ring_scatter(both, 2)
    columns = lax.axis_index("mat") * col_count + lax.iota(jnp.int32, col_count)
    block_ids = lax.iota(jnp.int32, local_blocks)
    column_pick = ((columns // per_block)[:, None] == block_ids[None, :]).astype(jnp.float32)
    row_pick = (
        (lax.iota(jnp.int32, block_orbs) // per_block)[:, None] == block_ids[None, :]
    ).astype(jnp.float32)
    select = jnp.einsum(
        "rkb,cb,ar->kca", correlation_pairs.astype(jnp.float32), column_pick, row_pick
    )
    return (gram_rows * select, energy_rows * select)


def solution(mesh):
    return jax.shard_map(
        on_device,
        mesh=mesh,
        in_specs=(
            P("dom", None, "mat", None),
            P("dom", "mat", None),
            P("dom"),
            P("dom"),
            P("dom"),
            P("dom", None, None),
        ),
        out_specs=(P(None, "mat", "dom"), P(None, "mat", "dom")),
        check_vma=False,
    )
```

```python
import jax
import jax.numpy as jnp
from jax import lax
from jax.sharding import PartitionSpec as P


def extended_2(array, sides, width):
    for axis, dim in sides:
        size, length = (lax.axis_size(axis), array.shape[dim])
        up = [(i, (i + 1) % size) for i in range(size)]
        down = [(j, i) for i, j in up]
        last = lax.slice_in_dim(array, length - width, length, axis=dim)
        first = lax.slice_in_dim(array, 0, width, axis=dim)
        before = lax.ppermute(last, axis, up)
        after = lax.ppermute(first, axis, down)
        array = jnp.concatenate([before, array, after], axis=dim)
    return array


def passed_along(block, axis, distance):
    devices = range(lax.axis_size(axis))
    route = [((i - distance) % len(devices), i) for i in devices]
    return lax.ppermute(block, axis, route)


def sphere_mask(
    centre_first,
    centre_second,
    centre_third,
    window_cells,
    patch_cells,
    second_cells,
    second_start,
    second_total,
    third_cells,
):
    planes = lax.iota(jnp.int32, window_cells)
    off_first = planes[None, :] - (patch_cells + centre_first[:, None])
    interior = (planes >= 1) & (planes <= window_cells - 2)
    second_coord = second_start + lax.iota(jnp.int32, second_cells)
    off_second = jnp.mod(second_coord[None, :] - centre_second[:, None], second_total)
    off_second = jnp.minimum(off_second, second_total - off_second)
    off_third = lax.iota(jnp.int32, third_cells)[None, :] - centre_third[:, None]
    radius = window_cells // 2
    distance = (
        (off_first * off_first)[:, :, None, None]
        + (off_second * off_second)[:, None, :, None]
        + (off_third * off_third)[:, None, None, :]
    )
    return (distance <= radius * radius) & interior[None, :, None, None]


def stencil(extended, potential_slab):
    centre_cells = extended[:, 1:-1, 1:-1, :].astype(jnp.float32)
    beside = extended[:, 2:, 1:-1, :].astype(jnp.float32) + extended[:, :-2, 1:-1, :].astype(
        jnp.float32
    )
    beside = (
        beside
        + extended[:, 1:-1, 2:, :].astype(jnp.float32)
        + extended[:, 1:-1, :-2, :].astype(jnp.float32)
    )
    third_padded = jnp.pad(centre_cells, ((0, 0), (0, 0), (0, 0), (1, 1)))
    beside = beside + third_padded[..., 2:] + third_padded[..., :-2]
    return 0.5 * (6.0 * centre_cells - beside) + potential_slab[None] * centre_cells


def pair_product(left, right):
    return lax.dot_general(
        left, right, (((1, 2, 3), (1, 2, 3)), ((), ())), preferred_element_type=jnp.float32
    )


def ring_scatter(full, axis):
    count = lax.axis_size("mat")
    me = lax.axis_index("mat")
    share = full.shape[axis] // count
    split = full.shape[-1] // 2
    halves = (full[..., :split], full[..., split:])
    forward = [(i, (i + 1) % count) for i in range(count)]
    backward = [((i + 1) % count, i) for i in range(count)]

    def chunk(values, index):
        return lax.dynamic_slice_in_dim(values, index * share, share, axis=axis)

    ahead = chunk(halves[0], lax.rem(me + count - 1, count))
    behind = chunk(halves[1], lax.rem(me + 1, count))
    for step in range(count - 1):
        ahead = lax.ppermute(ahead, "mat", forward)
        behind = lax.ppermute(behind, "mat", backward)
        ahead = ahead + chunk(halves[0], lax.rem(me + 2 * count - 2 - step, count))
        behind = behind + chunk(halves[1], lax.rem(me + 2 + step, count))
    return jnp.concatenate([ahead, behind], axis=-1)


def on_device(orbitals, potential, centre_first, centre_second, centre_third, correlation_pairs):
    block_orbs, window_cells, second_cells, third_cells = orbitals.shape
    patch_cells = potential.shape[0]
    local_blocks = correlation_pairs.shape[0]
    per_block = block_orbs // local_blocks
    mat_count = lax.axis_size("mat")
    second_start = lax.axis_index("mat") * second_cells
    inside = sphere_mask(
        centre_first,
        centre_second,
        centre_third,
        window_cells,
        patch_cells,
        second_cells,
        second_start,
        second_cells * mat_count,
        third_cells,
    )
    masked = jnp.where(inside, orbitals, jnp.zeros_like(orbitals))
    upper_start = 2 * patch_cells
    to_right = masked[:, upper_start - 1 : window_cells - 1]
    to_left = masked[:, 1 : patch_cells + 1]
    from_left = passed_along(to_right, "dom", 1)
    from_right = passed_along(to_left, "dom", -1)
    mat_size = lax.axis_size("mat")
    up = [(i, (i + 1) % mat_size) for i in range(mat_size)]
    down = [(j, i) for i, j in up]
    row_above = lax.ppermute(masked[:, :, second_cells - 1], "mat", up)
    row_below = lax.ppermute(masked[:, :, 0], "mat", down)
    rows_right = jnp.stack(
        [row_above[:, upper_start - 1 : window_cells - 1], row_below[:, upper_start - 1 : window_cells - 1]]
    )
    rows_left = jnp.stack([row_above[:, 1 : patch_cells + 1], row_below[:, 1 : patch_cells + 1]])
    rows_from_left = passed_along(rows_right, "dom", 1)
    rows_from_right = passed_along(rows_left, "dom", -1)

    def with_rows(planes, rows):
        return jnp.concatenate([rows[0][:, :, None], planes, rows[1][:, :, None]], axis=2)

    zero_plane = jnp.zeros_like(masked[:, :1])
    zero_rows = jnp.zeros((2, block_orbs, 1, third_cells), masked.dtype)
    own_ext = with_rows(
        masked[:, patch_cells - 1 : upper_start + 1],
        jnp.stack([row_above[:, patch_cells - 1 : upper_start + 1], row_below[:, patch_cells - 1 : upper_start + 1]]),
    )
    left_ext = with_rows(
        jnp.concatenate([from_left, zero_plane, zero_plane], axis=1),
        jnp.concatenate([rows_from_left, zero_rows, zero_rows], axis=2),
    )
    right_ext = with_rows(
        jnp.concatenate([zero_plane, zero_plane, from_right], axis=1),
        jnp.concatenate([zero_rows, zero_rows, rows_from_right], axis=2),
    )
    phi_slots = [
        jnp.concatenate([from_left[:, 1:], zero_plane], axis=1),
        masked[:, patch_cells:upper_start],
        jnp.concatenate([zero_plane, from_right[:, :-1]], axis=1),
    ]
    applied_slots = [
        stencil(ext, potential).astype(jnp.bfloat16) for ext in (left_ext, own_ext, right_ext)
    ]
    gram_full = jnp.stack(
        [jnp.stack([pair_product(phi_slots[a], phi_slots[b]) for b in range(3)], 1) for a in range(3)]
    )
    energy_full = jnp.stack(
        [
            jnp.stack([pair_product(applied_slots[a], phi_slots[b]) for b in range(3)], 1)
            for a in range(3)
        ]
    )
    col_count = block_orbs // mat_count

    def row_blocks(full):
        assembled = jnp.pad(full[:, :, 1], ((1, 1), (0, 0), (0, 0)))
        for slot_index, offset in ((0, -1), (2, 1)):
            arrived = passed_along(full[:, :, slot_index], "dom", offset)
            assembled = assembled + jnp.pad(arrived, ((2 - slot_index, slot_index), (0, 0), (0, 0)))
        return assembled

    gram_rows = ring_scatter(row_blocks(gram_full), 1)
    energy_rows = ring_scatter(row_blocks(energy_full), 1)
    columns = lax.axis_index("mat") * col_count + lax.iota(jnp.int32, col_count)
    block_ids = lax.iota(jnp.int32, local_blocks)
    column_pick = ((columns // per_block)[:, None] == block_ids[None, :]).astype(jnp.float32)
    row_pick = (
        (lax.iota(jnp.int32, block_orbs) // per_block)[:, None] == block_ids[None, :]
    ).astype(jnp.float32)
    select = jnp.einsum(
        "rkb,cb,ar->kca", correlation_pairs.astype(jnp.float32), column_pick, row_pick
    )
    return (gram_rows * select, energy_rows * select)


def solution(mesh):
    return jax.shard_map(
        on_device,
        mesh=mesh,
        in_specs=(
            P("dom", None, "mat", None),
            P("dom", "mat", None),
            P("dom"),
            P("dom"),
            P("dom"),
            P("dom", None, None),
        ),
        out_specs=(P(None, "mat", "dom"), P(None, "mat", "dom")),
        check_vma=False,
    )
```

```python
import jax
import jax.numpy as jnp
from jax import lax
from jax.sharding import PartitionSpec as P
from jax.experimental import pallas as pl
from jax.experimental.pallas import tpu as pltpu
import functools


def extended_2(array, sides, width):
    for axis, dim in sides:
        size, length = (lax.axis_size(axis), array.shape[dim])
        up = [(i, (i + 1) % size) for i in range(size)]
        down = [(j, i) for i, j in up]
        last = lax.slice_in_dim(array, length - width, length, axis=dim)
        first = lax.slice_in_dim(array, 0, width, axis=dim)
        before = lax.ppermute(last, axis, up)
        after = lax.ppermute(first, axis, down)
        array = jnp.concatenate([before, array, after], axis=dim)
    return array


def passed_along(block, axis, distance):
    devices = range(lax.axis_size(axis))
    route = [((i - distance) % len(devices), i) for i in devices]
    return lax.ppermute(block, axis, route)


def sphere_mask(
    centre_first,
    centre_second,
    centre_third,
    window_cells,
    patch_cells,
    second_cells,
    second_start,
    second_total,
    third_cells,
):
    planes = lax.iota(jnp.int32, window_cells)
    off_first = planes[None, :] - (patch_cells + centre_first[:, None])
    interior = (planes >= 1) & (planes <= window_cells - 2)
    second_coord = second_start + lax.iota(jnp.int32, second_cells)
    off_second = jnp.mod(second_coord[None, :] - centre_second[:, None], second_total)
    off_second = jnp.minimum(off_second, second_total - off_second)
    off_third = lax.iota(jnp.int32, third_cells)[None, :] - centre_third[:, None]
    radius = window_cells // 2
    distance = (
        (off_first * off_first)[:, :, None, None]
        + (off_second * off_second)[:, None, :, None]
        + (off_third * off_third)[:, None, None, :]
    )
    return (distance <= radius * radius) & interior[None, :, None, None]


def stencil(extended, potential_slab):
    centre_cells = extended[:, 1:-1, 1:-1, :].astype(jnp.float32)
    beside = extended[:, 2:, 1:-1, :].astype(jnp.float32) + extended[:, :-2, 1:-1, :].astype(
        jnp.float32
    )
    beside = (
        beside
        + extended[:, 1:-1, 2:, :].astype(jnp.float32)
        + extended[:, 1:-1, :-2, :].astype(jnp.float32)
    )
    third_padded = jnp.pad(centre_cells, ((0, 0), (0, 0), (0, 0), (1, 1)))
    beside = beside + third_padded[..., 2:] + third_padded[..., :-2]
    return 0.5 * (6.0 * centre_cells - beside) + potential_slab[None] * centre_cells


def pair_product(left, right):
    return lax.dot_general(
        left, right, (((1, 2, 3), (1, 2, 3)), ((), ())), preferred_element_type=jnp.float32
    )


def ring_scatter(full, axis):
    count = lax.axis_size("mat")
    me = lax.axis_index("mat")
    share = full.shape[axis] // count
    split = full.shape[-1] // 2
    halves = (full[..., :split], full[..., split:])
    forward = [(i, (i + 1) % count) for i in range(count)]
    backward = [((i + 1) % count, i) for i in range(count)]

    def chunk(values, index):
        return lax.dynamic_slice_in_dim(values, index * share, share, axis=axis)

    ahead = chunk(halves[0], lax.rem(me + count - 1, count))
    behind = chunk(halves[1], lax.rem(me + 1, count))
    for step in range(count - 1):
        ahead = lax.ppermute(ahead, "mat", forward)
        behind = lax.ppermute(behind, "mat", backward)
        ahead = ahead + chunk(halves[0], lax.rem(me + 2 * count - 2 - step, count))
        behind = behind + chunk(halves[1], lax.rem(me + 2 + step, count))
    return jnp.concatenate([ahead, behind], axis=-1)


def ring_kernel(count, share, half, x_ref, o_ref, stage_f, stage_b, land_f, land_b, send_f, recv_f, send_b, recv_b):
    me = lax.axis_index("mat")
    dom = lax.axis_index("dom")
    right = lax.rem(me + 1, count)
    left = lax.rem(me + count - 1, count)
    mesh_ids = pl.DeviceIdType.MESH
    barrier = pltpu.get_barrier_semaphore()
    for neighbour in (left, right):
        pl.semaphore_signal(barrier, 1, device_id=(dom, neighbour), device_id_type=mesh_ids)
    pl.semaphore_wait(barrier, 2)

    def own(index, low):
        start = pl.multiple_of(index * share, share)
        return x_ref[:, pl.ds(start, share), pl.ds(low, half)]

    stage_f[0] = own(lax.rem(me + count - 1, count), 0)
    stage_b[0] = own(lax.rem(me + 1, count), half)
    for step in range(count - 1):
        ahead = pltpu.make_async_remote_copy(
            src_ref=stage_f.at[step],
            dst_ref=land_f.at[step],
            send_sem=send_f.at[step],
            recv_sem=recv_f.at[step],
            device_id=(dom, right),
            device_id_type=mesh_ids,
        )
        behind = pltpu.make_async_remote_copy(
            src_ref=stage_b.at[step],
            dst_ref=land_b.at[step],
            send_sem=send_b.at[step],
            recv_sem=recv_b.at[step],
            device_id=(dom, left),
            device_id_type=mesh_ids,
        )
        ahead.start()
        behind.start()
        ahead.wait()
        behind.wait()
        forward_sum = land_f[step] + own(lax.rem(me + 2 * count - 2 - step, count), 0)
        backward_sum = land_b[step] + own(lax.rem(me + 2 + step, count), half)
        if step < count - 2:
            stage_f[step + 1] = forward_sum
            stage_b[step + 1] = backward_sum
        else:
            o_ref[:, :, pl.ds(0, half)] = forward_sum
            o_ref[:, :, pl.ds(half, half)] = backward_sum


def ring_scatter_kernel(full):
    count = lax.axis_size("mat")
    planes, rows, cols = full.shape
    share = rows // count
    half = cols // 2
    piece = pltpu.VMEM((count - 1, planes, share, half), jnp.float32)
    return pl.pallas_call(
        functools.partial(ring_kernel, count, share, half),
        out_shape=jax.ShapeDtypeStruct((planes, share, cols), jnp.float32),
        in_specs=[pl.BlockSpec(memory_space=pltpu.VMEM)],
        out_specs=pl.BlockSpec(memory_space=pltpu.VMEM),
        scratch_shapes=[piece, piece, piece, piece]
        + [pltpu.SemaphoreType.DMA((count - 1,))] * 4,
        compiler_params=pltpu.CompilerParams(collective_id=0, has_side_effects=True),
    )(full)


def on_device(orbitals, potential, centre_first, centre_second, centre_third, correlation_pairs):
    block_orbs, window_cells, second_cells, third_cells = orbitals.shape
    patch_cells = potential.shape[0]
    local_blocks = correlation_pairs.shape[0]
    per_block = block_orbs // local_blocks
    mat_count = lax.axis_size("mat")
    second_start = lax.axis_index("mat") * second_cells
    inside = sphere_mask(
        centre_first,
        centre_second,
        centre_third,
        window_cells,
        patch_cells,
        second_cells,
        second_start,
        second_cells * mat_count,
        third_cells,
    )
    masked = jnp.where(inside, orbitals, jnp.zeros_like(orbitals))
    upper_start = 2 * patch_cells
    to_right = masked[:, upper_start - 1 : window_cells - 1]
    to_left = masked[:, 1 : patch_cells + 1]
    from_left = passed_along(to_right, "dom", 1)
    from_right = passed_along(to_left, "dom", -1)
    mat_size = lax.axis_size("mat")
    up = [(i, (i + 1) % mat_size) for i in range(mat_size)]
    down = [(j, i) for i, j in up]
    row_above = lax.ppermute(masked[:, :, second_cells - 1], "mat", up)
    row_below = lax.ppermute(masked[:, :, 0], "mat", down)
    rows_right = jnp.stack(
        [row_above[:, upper_start - 1 : window_cells - 1], row_below[:, upper_start - 1 : window_cells - 1]]
    )
    rows_left = jnp.stack([row_above[:, 1 : patch_cells + 1], row_below[:, 1 : patch_cells + 1]])
    rows_from_left = passed_along(rows_right, "dom", 1)
    rows_from_right = passed_along(rows_left, "dom", -1)

    def with_rows(planes, rows):
        return jnp.concatenate([rows[0][:, :, None], planes, rows[1][:, :, None]], axis=2)

    zero_plane = jnp.zeros_like(masked[:, :1])
    zero_rows = jnp.zeros((2, block_orbs, 1, third_cells), masked.dtype)
    own_ext = with_rows(
        masked[:, patch_cells - 1 : upper_start + 1],
        jnp.stack([row_above[:, patch_cells - 1 : upper_start + 1], row_below[:, patch_cells - 1 : upper_start + 1]]),
    )
    left_ext = with_rows(
        jnp.concatenate([from_left, zero_plane, zero_plane], axis=1),
        jnp.concatenate([rows_from_left, zero_rows, zero_rows], axis=2),
    )
    right_ext = with_rows(
        jnp.concatenate([zero_plane, zero_plane, from_right], axis=1),
        jnp.concatenate([zero_rows, zero_rows, rows_from_right], axis=2),
    )
    phi_slots = [
        jnp.concatenate([from_left[:, 1:], zero_plane], axis=1),
        masked[:, patch_cells:upper_start],
        jnp.concatenate([zero_plane, from_right[:, :-1]], axis=1),
    ]
    applied_slots = [
        stencil(ext, potential).astype(jnp.bfloat16) for ext in (left_ext, own_ext, right_ext)
    ]
    gram_full = jnp.stack(
        [jnp.stack([pair_product(phi_slots[a], phi_slots[b]) for b in range(3)], 1) for a in range(3)]
    )
    energy_full = jnp.stack(
        [
            jnp.stack([pair_product(applied_slots[a], phi_slots[b]) for b in range(3)], 1)
            for a in range(3)
        ]
    )
    col_count = block_orbs // mat_count

    def row_blocks(full):
        assembled = jnp.pad(full[:, :, 1], ((1, 1), (0, 0), (0, 0)))
        for slot_index, offset in ((0, -1), (2, 1)):
            arrived = passed_along(full[:, :, slot_index], "dom", offset)
            assembled = assembled + jnp.pad(arrived, ((2 - slot_index, slot_index), (0, 0), (0, 0)))
        return assembled

    both = jnp.stack([row_blocks(gram_full), row_blocks(energy_full)])
    blocks = both.shape[:2]
    summed = ring_scatter_kernel(both.reshape((-1,) + both.shape[2:]))
    gram_rows, energy_rows = summed.reshape(blocks + summed.shape[1:])
    columns = lax.axis_index("mat") * col_count + lax.iota(jnp.int32, col_count)
    block_ids = lax.iota(jnp.int32, local_blocks)
    column_pick = ((columns // per_block)[:, None] == block_ids[None, :]).astype(jnp.float32)
    row_pick = (
        (lax.iota(jnp.int32, block_orbs) // per_block)[:, None] == block_ids[None, :]
    ).astype(jnp.float32)
    select = jnp.einsum(
        "rkb,cb,ar->kca", correlation_pairs.astype(jnp.float32), column_pick, row_pick
    )
    return (gram_rows * select, energy_rows * select)


def solution(mesh):
    return jax.shard_map(
        on_device,
        mesh=mesh,
        in_specs=(
            P("dom", None, "mat", None),
            P("dom", "mat", None),
            P("dom"),
            P("dom"),
            P("dom"),
            P("dom", None, None),
        ),
        out_specs=(P(None, "mat", "dom"), P(None, "mat", "dom")),
        check_vma=False,
    )
```

```python
import jax
import jax.numpy as jnp
from jax import lax
from jax.sharding import PartitionSpec as P
from jax.experimental import pallas as pl
from jax.experimental.pallas import tpu as pltpu
import functools


def extended_2(array, sides, width):
    for axis, dim in sides:
        size, length = (lax.axis_size(axis), array.shape[dim])
        up = [(i, (i + 1) % size) for i in range(size)]
        down = [(j, i) for i, j in up]
        last = lax.slice_in_dim(array, length - width, length, axis=dim)
        first = lax.slice_in_dim(array, 0, width, axis=dim)
        before = lax.ppermute(last, axis, up)
        after = lax.ppermute(first, axis, down)
        array = jnp.concatenate([before, array, after], axis=dim)
    return array


def passed_along(block, axis, distance):
    devices = range(lax.axis_size(axis))
    route = [((i - distance) % len(devices), i) for i in devices]
    return lax.ppermute(block, axis, route)


def sphere_mask(
    centre_first,
    centre_second,
    centre_third,
    window_cells,
    patch_cells,
    second_cells,
    second_start,
    second_total,
    third_cells,
):
    planes = lax.iota(jnp.int32, window_cells)
    off_first = planes[None, :] - (patch_cells + centre_first[:, None])
    interior = (planes >= 1) & (planes <= window_cells - 2)
    second_coord = second_start + lax.iota(jnp.int32, second_cells)
    off_second = jnp.mod(second_coord[None, :] - centre_second[:, None], second_total)
    off_second = jnp.minimum(off_second, second_total - off_second)
    off_third = lax.iota(jnp.int32, third_cells)[None, :] - centre_third[:, None]
    radius = window_cells // 2
    distance = (
        (off_first * off_first)[:, :, None, None]
        + (off_second * off_second)[:, None, :, None]
        + (off_third * off_third)[:, None, None, :]
    )
    return (distance <= radius * radius) & interior[None, :, None, None]


def stencil(extended, potential_slab):
    centre_cells = extended[:, 1:-1, 1:-1, :].astype(jnp.float32)
    beside = extended[:, 2:, 1:-1, :].astype(jnp.float32) + extended[:, :-2, 1:-1, :].astype(
        jnp.float32
    )
    beside = (
        beside
        + extended[:, 1:-1, 2:, :].astype(jnp.float32)
        + extended[:, 1:-1, :-2, :].astype(jnp.float32)
    )
    third_padded = jnp.pad(centre_cells, ((0, 0), (0, 0), (0, 0), (1, 1)))
    beside = beside + third_padded[..., 2:] + third_padded[..., :-2]
    return 0.5 * (6.0 * centre_cells - beside) + potential_slab[None] * centre_cells


def pair_product(left, right):
    return lax.dot_general(
        left, right, (((1, 2, 3), (1, 2, 3)), ((), ())), preferred_element_type=jnp.float32
    )


def ring_scatter(full, axis):
    count = lax.axis_size("mat")
    me = lax.axis_index("mat")
    share = full.shape[axis] // count
    split = full.shape[-1] // 2
    halves = (full[..., :split], full[..., split:])
    forward = [(i, (i + 1) % count) for i in range(count)]
    backward = [((i + 1) % count, i) for i in range(count)]

    def chunk(values, index):
        return lax.dynamic_slice_in_dim(values, index * share, share, axis=axis)

    ahead = chunk(halves[0], lax.rem(me + count - 1, count))
    behind = chunk(halves[1], lax.rem(me + 1, count))
    for step in range(count - 1):
        ahead = lax.ppermute(ahead, "mat", forward)
        behind = lax.ppermute(behind, "mat", backward)
        ahead = ahead + chunk(halves[0], lax.rem(me + 2 * count - 2 - step, count))
        behind = behind + chunk(halves[1], lax.rem(me + 2 + step, count))
    return jnp.concatenate([ahead, behind], axis=-1)


def ring_kernel(count, share, half, x_ref, o_ref, stage_f, stage_b, land_f, land_b, send_f, recv_f, send_b, recv_b):
    me = lax.axis_index("mat")
    dom = lax.axis_index("dom")
    right = lax.rem(me + 1, count)
    left = lax.rem(me + count - 1, count)
    mesh_ids = pl.DeviceIdType.MESH
    barrier = pltpu.get_barrier_semaphore()
    for neighbour in (left, right):
        pl.semaphore_signal(barrier, 1, device_id=(dom, neighbour), device_id_type=mesh_ids)
    pl.semaphore_wait(barrier, 2)

    def own(index, low):
        start = pl.multiple_of(index * share, share)
        return x_ref[:, pl.ds(start, share), pl.ds(low, half)]

    stage_f[0] = own(lax.rem(me + count - 1, count), 0)
    stage_b[0] = own(lax.rem(me + 1, count), half)
    for step in range(count - 1):
        ahead = pltpu.make_async_remote_copy(
            src_ref=stage_f.at[step],
            dst_ref=land_f.at[step],
            send_sem=send_f.at[step],
            recv_sem=recv_f.at[step],
            device_id=(dom, right),
            device_id_type=mesh_ids,
        )
        behind = pltpu.make_async_remote_copy(
            src_ref=stage_b.at[step],
            dst_ref=land_b.at[step],
            send_sem=send_b.at[step],
            recv_sem=recv_b.at[step],
            device_id=(dom, left),
            device_id_type=mesh_ids,
        )
        ahead.start()
        behind.start()
        ahead.wait()
        behind.wait()
        forward_sum = land_f[step] + own(lax.rem(me + 2 * count - 2 - step, count), 0)
        backward_sum = land_b[step] + own(lax.rem(me + 2 + step, count), half)
        if step < count - 2:
            stage_f[step + 1] = forward_sum
            stage_b[step + 1] = backward_sum
        else:
            o_ref[:, :, pl.ds(0, half)] = forward_sum
            o_ref[:, :, pl.ds(half, half)] = backward_sum


def ring_scatter_kernel(full):
    count = lax.axis_size("mat")
    planes, rows, cols = full.shape
    share = rows // count
    half = cols // 2
    piece = pltpu.VMEM((count - 1, planes, share, half), jnp.float32)
    return pl.pallas_call(
        functools.partial(ring_kernel, count, share, half),
        out_shape=jax.ShapeDtypeStruct((planes, share, cols), jnp.float32),
        in_specs=[pl.BlockSpec(memory_space=pltpu.VMEM)],
        out_specs=pl.BlockSpec(memory_space=pltpu.VMEM),
        scratch_shapes=[piece, piece, piece, piece]
        + [pltpu.SemaphoreType.DMA((count - 1,))] * 4,
        compiler_params=pltpu.CompilerParams(collective_id=0, has_side_effects=True),
    )(full)


def on_device(orbitals, potential, centre_first, centre_second, centre_third, correlation_pairs):
    block_orbs, window_cells, second_cells, third_cells = orbitals.shape
    patch_cells = potential.shape[0]
    local_blocks = correlation_pairs.shape[0]
    per_block = block_orbs // local_blocks
    mat_count = lax.axis_size("mat")
    second_start = lax.axis_index("mat") * second_cells
    inside = sphere_mask(
        centre_first,
        centre_second,
        centre_third,
        window_cells,
        patch_cells,
        second_cells,
        second_start,
        second_cells * mat_count,
        third_cells,
    )
    masked = jnp.where(inside, orbitals, jnp.zeros_like(orbitals))
    upper_start = 2 * patch_cells
    to_right = masked[:, upper_start - 1 : window_cells - 1]
    to_left = masked[:, 1 : patch_cells + 1]
    from_left = passed_along(to_right, "dom", 1)
    from_right = passed_along(to_left, "dom", -1)
    mat_size = lax.axis_size("mat")
    up = [(i, (i + 1) % mat_size) for i in range(mat_size)]
    down = [(j, i) for i, j in up]
    row_above = lax.ppermute(masked[:, :, second_cells - 1], "mat", up)
    row_below = lax.ppermute(masked[:, :, 0], "mat", down)
    rows_right = jnp.stack(
        [row_above[:, upper_start - 1 : window_cells - 1], row_below[:, upper_start - 1 : window_cells - 1]]
    )
    rows_left = jnp.stack([row_above[:, 1 : patch_cells + 1], row_below[:, 1 : patch_cells + 1]])
    rows_from_left = passed_along(rows_right, "dom", 1)
    rows_from_right = passed_along(rows_left, "dom", -1)

    def with_rows(planes, rows):
        return jnp.concatenate([rows[0][:, :, None], planes, rows[1][:, :, None]], axis=2)

    zero_plane = jnp.zeros_like(masked[:, :1])
    zero_rows = jnp.zeros((2, block_orbs, 1, third_cells), masked.dtype)
    own_ext = with_rows(
        masked[:, patch_cells - 1 : upper_start + 1],
        jnp.stack([row_above[:, patch_cells - 1 : upper_start + 1], row_below[:, patch_cells - 1 : upper_start + 1]]),
    )
    left_ext = with_rows(
        jnp.concatenate([from_left, zero_plane, zero_plane], axis=1),
        jnp.concatenate([rows_from_left, zero_rows, zero_rows], axis=2),
    )
    right_ext = with_rows(
        jnp.concatenate([zero_plane, zero_plane, from_right], axis=1),
        jnp.concatenate([zero_rows, zero_rows, rows_from_right], axis=2),
    )
    phi_slots = [
        jnp.concatenate([from_left[:, 1:], zero_plane], axis=1),
        masked[:, patch_cells:upper_start],
        jnp.concatenate([zero_plane, from_right[:, :-1]], axis=1),
    ]
    gram_full = jnp.stack(
        [jnp.stack([pair_product(phi_slots[a], phi_slots[b]) for b in range(3)], 1) for a in range(3)]
    )
    gram_full, left_ext, right_ext = lax.optimization_barrier((gram_full, left_ext, right_ext))
    applied_slots = [
        stencil(ext, potential).astype(jnp.bfloat16) for ext in (left_ext, own_ext, right_ext)
    ]
    energy_full = jnp.stack(
        [
            jnp.stack([pair_product(applied_slots[a], phi_slots[b]) for b in range(3)], 1)
            for a in range(3)
        ]
    )
    col_count = block_orbs // mat_count

    def row_blocks(full):
        assembled = jnp.pad(full[:, :, 1], ((1, 1), (0, 0), (0, 0)))
        for slot_index, offset in ((0, -1), (2, 1)):
            arrived = passed_along(full[:, :, slot_index], "dom", offset)
            assembled = assembled + jnp.pad(arrived, ((2 - slot_index, slot_index), (0, 0), (0, 0)))
        return assembled

    both = jnp.stack([row_blocks(gram_full), row_blocks(energy_full)])
    blocks = both.shape[:2]
    summed = ring_scatter_kernel(both.reshape((-1,) + both.shape[2:]))
    gram_rows, energy_rows = summed.reshape(blocks + summed.shape[1:])
    columns = lax.axis_index("mat") * col_count + lax.iota(jnp.int32, col_count)
    block_ids = lax.iota(jnp.int32, local_blocks)
    column_pick = ((columns // per_block)[:, None] == block_ids[None, :]).astype(jnp.float32)
    row_pick = (
        (lax.iota(jnp.int32, block_orbs) // per_block)[:, None] == block_ids[None, :]
    ).astype(jnp.float32)
    select = jnp.einsum(
        "rkb,cb,ar->kca", correlation_pairs.astype(jnp.float32), column_pick, row_pick
    )
    return (gram_rows * select, energy_rows * select)


def solution(mesh):
    return jax.shard_map(
        on_device,
        mesh=mesh,
        in_specs=(
            P("dom", None, "mat", None),
            P("dom", "mat", None),
            P("dom"),
            P("dom"),
            P("dom"),
            P("dom", None, None),
        ),
        out_specs=(P(None, "mat", "dom"), P(None, "mat", "dom")),
        check_vma=False,
    )
```

```python
import jax
import jax.numpy as jnp
from jax import lax
from jax.sharding import PartitionSpec as P
from jax.experimental import pallas as pl
from jax.experimental.pallas import tpu as pltpu
import functools


def extended_2(array, sides, width):
    for axis, dim in sides:
        size, length = (lax.axis_size(axis), array.shape[dim])
        up = [(i, (i + 1) % size) for i in range(size)]
        down = [(j, i) for i, j in up]
        last = lax.slice_in_dim(array, length - width, length, axis=dim)
        first = lax.slice_in_dim(array, 0, width, axis=dim)
        before = lax.ppermute(last, axis, up)
        after = lax.ppermute(first, axis, down)
        array = jnp.concatenate([before, array, after], axis=dim)
    return array


def passed_along(block, axis, distance):
    devices = range(lax.axis_size(axis))
    route = [((i - distance) % len(devices), i) for i in devices]
    return lax.ppermute(block, axis, route)


def sphere_mask(
    centre_first,
    centre_second,
    centre_third,
    window_cells,
    patch_cells,
    second_cells,
    second_start,
    second_total,
    third_cells,
):
    planes = lax.iota(jnp.int32, window_cells)
    off_first = planes[None, :] - (patch_cells + centre_first[:, None])
    interior = (planes >= 1) & (planes <= window_cells - 2)
    second_coord = second_start + lax.iota(jnp.int32, second_cells)
    off_second = jnp.mod(second_coord[None, :] - centre_second[:, None], second_total)
    off_second = jnp.minimum(off_second, second_total - off_second)
    off_third = lax.iota(jnp.int32, third_cells)[None, :] - centre_third[:, None]
    radius = window_cells // 2
    distance = (
        (off_first * off_first)[:, :, None, None]
        + (off_second * off_second)[:, None, :, None]
        + (off_third * off_third)[:, None, None, :]
    )
    return (distance <= radius * radius) & interior[None, :, None, None]


def stencil(extended, potential_slab):
    centre_cells = extended[:, 1:-1, 1:-1, :].astype(jnp.float32)
    beside = extended[:, 2:, 1:-1, :].astype(jnp.float32) + extended[:, :-2, 1:-1, :].astype(
        jnp.float32
    )
    beside = (
        beside
        + extended[:, 1:-1, 2:, :].astype(jnp.float32)
        + extended[:, 1:-1, :-2, :].astype(jnp.float32)
    )
    third_padded = jnp.pad(centre_cells, ((0, 0), (0, 0), (0, 0), (1, 1)))
    beside = beside + third_padded[..., 2:] + third_padded[..., :-2]
    return 0.5 * (6.0 * centre_cells - beside) + potential_slab[None] * centre_cells


def pair_product(left, right):
    return lax.dot_general(
        left, right, (((1, 2, 3), (1, 2, 3)), ((), ())), preferred_element_type=jnp.float32
    )


def ring_scatter(full, axis):
    count = lax.axis_size("mat")
    me = lax.axis_index("mat")
    share = full.shape[axis] // count
    split = full.shape[-1] // 2
    halves = (full[..., :split], full[..., split:])
    forward = [(i, (i + 1) % count) for i in range(count)]
    backward = [((i + 1) % count, i) for i in range(count)]

    def chunk(values, index):
        return lax.dynamic_slice_in_dim(values, index * share, share, axis=axis)

    ahead = chunk(halves[0], lax.rem(me + count - 1, count))
    behind = chunk(halves[1], lax.rem(me + 1, count))
    for step in range(count - 1):
        ahead = lax.ppermute(ahead, "mat", forward)
        behind = lax.ppermute(behind, "mat", backward)
        ahead = ahead + chunk(halves[0], lax.rem(me + 2 * count - 2 - step, count))
        behind = behind + chunk(halves[1], lax.rem(me + 2 + step, count))
    return jnp.concatenate([ahead, behind], axis=-1)


def exchange_kernel(
    count, domains, share, half, x_ref, o_ref, total, from_left, from_right, stage_f, stage_b,
    land_f, land_b, dom_send, dom_recv, send_f, recv_f, send_b, recv_b,
):
    me = lax.axis_index("mat")
    dom = lax.axis_index("dom")
    right = lax.rem(me + 1, count)
    left = lax.rem(me + count - 1, count)
    up = lax.rem(dom + 1, domains)
    down = lax.rem(dom + domains - 1, domains)
    mesh_ids = pl.DeviceIdType.MESH
    barrier = pltpu.get_barrier_semaphore()
    for device in ((dom, left), (dom, right), (down, me), (up, me)):
        pl.semaphore_signal(barrier, 1, device_id=device, device_id_type=mesh_ids)
    pl.semaphore_wait(barrier, 4)

    to_down = pltpu.make_async_remote_copy(
        src_ref=x_ref.at[0],
        dst_ref=from_right,
        send_sem=dom_send.at[0],
        recv_sem=dom_recv.at[0],
        device_id=(down, me),
        device_id_type=mesh_ids,
    )
    to_up = pltpu.make_async_remote_copy(
        src_ref=x_ref.at[2],
        dst_ref=from_left,
        send_sem=dom_send.at[1],
        recv_sem=dom_recv.at[1],
        device_id=(up, me),
        device_id_type=mesh_ids,
    )
    to_down.start()
    to_up.start()
    to_down.wait()
    to_up.wait()
    total[:, 0] = from_left[:, 0]
    total[:, 1] = from_left[:, 1] + x_ref[1, :, 0]
    total[:, 2] = from_left[:, 2] + x_ref[1, :, 1] + from_right[:, 0]
    total[:, 3] = x_ref[1, :, 2] + from_right[:, 1]
    total[:, 4] = from_right[:, 2]

    def own(index, low):
        start = pl.multiple_of(index * share, share)
        return total[:, :, pl.ds(start, share), pl.ds(low, half)]

    stage_f[0] = own(lax.rem(me + count - 1, count), 0)
    stage_b[0] = own(lax.rem(me + 1, count), half)
    for step in range(count - 1):
        ahead = pltpu.make_async_remote_copy(
            src_ref=stage_f.at[step],
            dst_ref=land_f.at[step],
            send_sem=send_f.at[step],
            recv_sem=recv_f.at[step],
            device_id=(dom, right),
            device_id_type=mesh_ids,
        )
        behind = pltpu.make_async_remote_copy(
            src_ref=stage_b.at[step],
            dst_ref=land_b.at[step],
            send_sem=send_b.at[step],
            recv_sem=recv_b.at[step],
            device_id=(dom, left),
            device_id_type=mesh_ids,
        )
        ahead.start()
        behind.start()
        ahead.wait()
        behind.wait()
        forward_sum = land_f[step] + own(lax.rem(me + 2 * count - 2 - step, count), 0)
        backward_sum = land_b[step] + own(lax.rem(me + 2 + step, count), half)
        if step < count - 2:
            stage_f[step + 1] = forward_sum
            stage_b[step + 1] = backward_sum
        else:
            o_ref[:, :, :, pl.ds(0, half)] = forward_sum
            o_ref[:, :, :, pl.ds(half, half)] = backward_sum


def exchange_and_sum(full):
    count = lax.axis_size("mat")
    domains = lax.axis_size("dom")
    slots, outputs, columns, rows, cols = full.shape
    share = rows // count
    half = cols // 2
    piece = pltpu.VMEM((count - 1, outputs, 2 * columns - 1, share, half), jnp.float32)
    arrived = pltpu.VMEM((outputs, columns, rows, cols), jnp.float32)
    return pl.pallas_call(
        functools.partial(exchange_kernel, count, domains, share, half),
        out_shape=jax.ShapeDtypeStruct((outputs, 2 * columns - 1, share, cols), jnp.float32),
        in_specs=[pl.BlockSpec(memory_space=pltpu.VMEM)],
        out_specs=pl.BlockSpec(memory_space=pltpu.VMEM),
        scratch_shapes=[
            pltpu.VMEM((outputs, 2 * columns - 1, rows, cols), jnp.float32),
            arrived,
            arrived,
            piece,
            piece,
            piece,
            piece,
        ]
        + [pltpu.SemaphoreType.DMA((2,))] * 2
        + [pltpu.SemaphoreType.DMA((count - 1,))] * 4,
        compiler_params=pltpu.CompilerParams(
            collective_id=0, has_side_effects=True, vmem_limit_bytes=48 * 1024 * 1024
        ),
    )(full)


def on_device(orbitals, potential, centre_first, centre_second, centre_third, correlation_pairs):
    block_orbs, window_cells, second_cells, third_cells = orbitals.shape
    patch_cells = potential.shape[0]
    local_blocks = correlation_pairs.shape[0]
    per_block = block_orbs // local_blocks
    mat_count = lax.axis_size("mat")
    second_start = lax.axis_index("mat") * second_cells
    inside = sphere_mask(
        centre_first,
        centre_second,
        centre_third,
        window_cells,
        patch_cells,
        second_cells,
        second_start,
        second_cells * mat_count,
        third_cells,
    )
    masked = jnp.where(inside, orbitals, jnp.zeros_like(orbitals))
    upper_start = 2 * patch_cells
    to_right = masked[:, upper_start - 1 : window_cells - 1]
    to_left = masked[:, 1 : patch_cells + 1]
    from_left = passed_along(to_right, "dom", 1)
    from_right = passed_along(to_left, "dom", -1)
    mat_size = lax.axis_size("mat")
    up = [(i, (i + 1) % mat_size) for i in range(mat_size)]
    down = [(j, i) for i, j in up]
    row_above = lax.ppermute(masked[:, :, second_cells - 1], "mat", up)
    row_below = lax.ppermute(masked[:, :, 0], "mat", down)
    rows_right = jnp.stack(
        [row_above[:, upper_start - 1 : window_cells - 1], row_below[:, upper_start - 1 : window_cells - 1]]
    )
    rows_left = jnp.stack([row_above[:, 1 : patch_cells + 1], row_below[:, 1 : patch_cells + 1]])
    rows_from_left = passed_along(rows_right, "dom", 1)
    rows_from_right = passed_along(rows_left, "dom", -1)

    def with_rows(planes, rows):
        return jnp.concatenate([rows[0][:, :, None], planes, rows[1][:, :, None]], axis=2)

    zero_plane = jnp.zeros_like(masked[:, :1])
    zero_rows = jnp.zeros((2, block_orbs, 1, third_cells), masked.dtype)
    own_ext = with_rows(
        masked[:, patch_cells - 1 : upper_start + 1],
        jnp.stack([row_above[:, patch_cells - 1 : upper_start + 1], row_below[:, patch_cells - 1 : upper_start + 1]]),
    )
    left_ext = with_rows(
        jnp.concatenate([from_left, zero_plane, zero_plane], axis=1),
        jnp.concatenate([rows_from_left, zero_rows, zero_rows], axis=2),
    )
    right_ext = with_rows(
        jnp.concatenate([zero_plane, zero_plane, from_right], axis=1),
        jnp.concatenate([zero_rows, zero_rows, rows_from_right], axis=2),
    )
    phi_slots = [
        jnp.concatenate([from_left[:, 1:], zero_plane], axis=1),
        masked[:, patch_cells:upper_start],
        jnp.concatenate([zero_plane, from_right[:, :-1]], axis=1),
    ]
    applied_slots = [
        stencil(ext, potential).astype(jnp.bfloat16) for ext in (left_ext, own_ext, right_ext)
    ]
    full = jnp.stack(
        [
            jnp.stack(
                [
                    jnp.stack([pair_product(phi_slots[a], phi_slots[b]) for a in range(3)]),
                    jnp.stack([pair_product(applied_slots[a], phi_slots[b]) for a in range(3)]),
                ]
            )
            for b in range(3)
        ]
    )
    col_count = block_orbs // mat_count
    gram_rows, energy_rows = exchange_and_sum(full)
    columns = lax.axis_index("mat") * col_count + lax.iota(jnp.int32, col_count)
    block_ids = lax.iota(jnp.int32, local_blocks)
    column_pick = ((columns // per_block)[:, None] == block_ids[None, :]).astype(jnp.float32)
    row_pick = (
        (lax.iota(jnp.int32, block_orbs) // per_block)[:, None] == block_ids[None, :]
    ).astype(jnp.float32)
    select = jnp.einsum(
        "rkb,cb,ar->kca", correlation_pairs.astype(jnp.float32), column_pick, row_pick
    )
    return (gram_rows * select, energy_rows * select)


def solution(mesh):
    return jax.shard_map(
        on_device,
        mesh=mesh,
        in_specs=(
            P("dom", None, "mat", None),
            P("dom", "mat", None),
            P("dom"),
            P("dom"),
            P("dom"),
            P("dom", None, None),
        ),
        out_specs=(P(None, "mat", "dom"), P(None, "mat", "dom")),
        check_vma=False,
    )
```

```python
import jax
import jax.numpy as jnp
from jax import lax
from jax.sharding import PartitionSpec as P
from jax.experimental import pallas as pl
from jax.experimental.pallas import tpu as pltpu
import functools


def extended_2(array, sides, width):
    for axis, dim in sides:
        size, length = (lax.axis_size(axis), array.shape[dim])
        up = [(i, (i + 1) % size) for i in range(size)]
        down = [(j, i) for i, j in up]
        last = lax.slice_in_dim(array, length - width, length, axis=dim)
        first = lax.slice_in_dim(array, 0, width, axis=dim)
        before = lax.ppermute(last, axis, up)
        after = lax.ppermute(first, axis, down)
        array = jnp.concatenate([before, array, after], axis=dim)
    return array


def passed_along(block, axis, distance):
    devices = range(lax.axis_size(axis))
    route = [((i - distance) % len(devices), i) for i in devices]
    return lax.ppermute(block, axis, route)


def sphere_mask(
    centre_first,
    centre_second,
    centre_third,
    window_cells,
    patch_cells,
    second_cells,
    second_start,
    second_total,
    third_cells,
):
    planes = lax.iota(jnp.int32, window_cells)
    off_first = planes[None, :] - (patch_cells + centre_first[:, None])
    interior = (planes >= 1) & (planes <= window_cells - 2)
    second_coord = second_start + lax.iota(jnp.int32, second_cells)
    off_second = jnp.mod(second_coord[None, :] - centre_second[:, None], second_total)
    off_second = jnp.minimum(off_second, second_total - off_second)
    off_third = lax.iota(jnp.int32, third_cells)[None, :] - centre_third[:, None]
    radius = window_cells // 2
    distance = (
        (off_first * off_first)[:, :, None, None]
        + (off_second * off_second)[:, None, :, None]
        + (off_third * off_third)[:, None, None, :]
    )
    return (distance <= radius * radius) & interior[None, :, None, None]


def stencil(extended, potential_slab):
    centre_cells = extended[:, 1:-1, 1:-1, :].astype(jnp.float32)
    beside = extended[:, 2:, 1:-1, :].astype(jnp.float32) + extended[:, :-2, 1:-1, :].astype(
        jnp.float32
    )
    beside = (
        beside
        + extended[:, 1:-1, 2:, :].astype(jnp.float32)
        + extended[:, 1:-1, :-2, :].astype(jnp.float32)
    )
    third_padded = jnp.pad(centre_cells, ((0, 0), (0, 0), (0, 0), (1, 1)))
    beside = beside + third_padded[..., 2:] + third_padded[..., :-2]
    return 0.5 * (6.0 * centre_cells - beside) + potential_slab[None] * centre_cells


def pair_product(left, right):
    return lax.dot_general(
        left, right, (((1, 2, 3), (1, 2, 3)), ((), ())), preferred_element_type=jnp.float32
    )


def ring_scatter(full, axis):
    count = lax.axis_size("mat")
    me = lax.axis_index("mat")
    share = full.shape[axis] // count
    split = full.shape[-1] // 2
    halves = (full[..., :split], full[..., split:])
    forward = [(i, (i + 1) % count) for i in range(count)]
    backward = [((i + 1) % count, i) for i in range(count)]

    def chunk(values, index):
        return lax.dynamic_slice_in_dim(values, index * share, share, axis=axis)

    ahead = chunk(halves[0], lax.rem(me + count - 1, count))
    behind = chunk(halves[1], lax.rem(me + 1, count))
    for step in range(count - 1):
        ahead = lax.ppermute(ahead, "mat", forward)
        behind = lax.ppermute(behind, "mat", backward)
        ahead = ahead + chunk(halves[0], lax.rem(me + 2 * count - 2 - step, count))
        behind = behind + chunk(halves[1], lax.rem(me + 2 + step, count))
    return jnp.concatenate([ahead, behind], axis=-1)


def exchange_kernel(
    count, domains, share, half, x_ref, o_ref, total, from_left, from_right, stage_f, stage_b,
    land_f, land_b, dom_send, dom_recv, send_f, recv_f, send_b, recv_b,
):
    me = lax.axis_index("mat")
    dom = lax.axis_index("dom")
    right = lax.rem(me + 1, count)
    left = lax.rem(me + count - 1, count)
    up = lax.rem(dom + 1, domains)
    down = lax.rem(dom + domains - 1, domains)
    mesh_ids = pl.DeviceIdType.MESH
    barrier = pltpu.get_barrier_semaphore()
    for device in ((dom, left), (dom, right), (down, me), (up, me)):
        pl.semaphore_signal(barrier, 1, device_id=device, device_id_type=mesh_ids)
    pl.semaphore_wait(barrier, 4)

    exchanges = []
    for part in range(2):
        low = part * half
        to_down = pltpu.make_async_remote_copy(
            src_ref=x_ref.at[0, :, :, :, pl.ds(low, half)],
            dst_ref=from_right.at[part],
            send_sem=dom_send.at[2 * part],
            recv_sem=dom_recv.at[2 * part],
            device_id=(down, me),
            device_id_type=mesh_ids,
        )
        to_up = pltpu.make_async_remote_copy(
            src_ref=x_ref.at[2, :, :, :, pl.ds(low, half)],
            dst_ref=from_left.at[part],
            send_sem=dom_send.at[2 * part + 1],
            recv_sem=dom_recv.at[2 * part + 1],
            device_id=(up, me),
            device_id_type=mesh_ids,
        )
        to_down.start()
        to_up.start()
        exchanges.append((to_down, to_up))

    for part in range(2):
        low = part * half
        for copy in exchanges[part]:
            copy.wait()
        lefts, rights = from_left.at[part], from_right.at[part]
        here = total.at[part]
        here[:, 0] = lefts[:, 0]
        here[:, 1] = lefts[:, 1] + x_ref[1, :, 0, :, pl.ds(low, half)]
        here[:, 2] = lefts[:, 2] + x_ref[1, :, 1, :, pl.ds(low, half)] + rights[:, 0]
        here[:, 3] = x_ref[1, :, 2, :, pl.ds(low, half)] + rights[:, 1]
        here[:, 4] = rights[:, 2]

        def own(output, index):
            start = pl.multiple_of(index * share, share)
            return here[output, :, pl.ds(start, share), :]

        stage_f[part, 0] = own(0, lax.rem(me + count - 1, count))
        stage_b[part, 0] = own(1, lax.rem(me + 1, count))
        for step in range(count - 1):
            slot = part * (count - 1) + step
            ahead = pltpu.make_async_remote_copy(
                src_ref=stage_f.at[part, step],
                dst_ref=land_f.at[part, step],
                send_sem=send_f.at[slot],
                recv_sem=recv_f.at[slot],
                device_id=(dom, right),
                device_id_type=mesh_ids,
            )
            behind = pltpu.make_async_remote_copy(
                src_ref=stage_b.at[part, step],
                dst_ref=land_b.at[part, step],
                send_sem=send_b.at[slot],
                recv_sem=recv_b.at[slot],
                device_id=(dom, left),
                device_id_type=mesh_ids,
            )
            ahead.start()
            behind.start()
            ahead.wait()
            behind.wait()
            forward_sum = land_f[part, step] + own(0, lax.rem(me + 2 * count - 2 - step, count))
            backward_sum = land_b[part, step] + own(1, lax.rem(me + 2 + step, count))
            if step < count - 2:
                stage_f[part, step + 1] = forward_sum
                stage_b[part, step + 1] = backward_sum
            else:
                o_ref[0, :, :, pl.ds(low, half)] = forward_sum
                o_ref[1, :, :, pl.ds(low, half)] = backward_sum


def exchange_and_sum(full):
    count = lax.axis_size("mat")
    domains = lax.axis_size("dom")
    slots, outputs, columns, rows, cols = full.shape
    share = rows // count
    half = cols // 2
    offsets = 2 * columns - 1
    piece = pltpu.VMEM((2, count - 1, offsets, share, half), jnp.float32)
    arrived = pltpu.VMEM((2, outputs, columns, rows, half), jnp.float32)
    return pl.pallas_call(
        functools.partial(exchange_kernel, count, domains, share, half),
        out_shape=jax.ShapeDtypeStruct((outputs, offsets, share, cols), jnp.float32),
        in_specs=[pl.BlockSpec(memory_space=pltpu.VMEM)],
        out_specs=pl.BlockSpec(memory_space=pltpu.VMEM),
        scratch_shapes=[
            pltpu.VMEM((2, outputs, offsets, rows, half), jnp.float32),
            arrived,
            arrived,
            piece,
            piece,
            piece,
            piece,
        ]
        + [pltpu.SemaphoreType.DMA((4,))] * 2
        + [pltpu.SemaphoreType.DMA((2 * (count - 1),))] * 4,
        compiler_params=pltpu.CompilerParams(
            collective_id=0, has_side_effects=True, vmem_limit_bytes=48 * 1024 * 1024
        ),
    )(full)


def on_device(orbitals, potential, centre_first, centre_second, centre_third, correlation_pairs):
    block_orbs, window_cells, second_cells, third_cells = orbitals.shape
    patch_cells = potential.shape[0]
    local_blocks = correlation_pairs.shape[0]
    per_block = block_orbs // local_blocks
    mat_count = lax.axis_size("mat")
    second_start = lax.axis_index("mat") * second_cells
    inside = sphere_mask(
        centre_first,
        centre_second,
        centre_third,
        window_cells,
        patch_cells,
        second_cells,
        second_start,
        second_cells * mat_count,
        third_cells,
    )
    masked = jnp.where(inside, orbitals, jnp.zeros_like(orbitals))
    upper_start = 2 * patch_cells
    to_right = masked[:, upper_start - 1 : window_cells - 1]
    to_left = masked[:, 1 : patch_cells + 1]
    from_left = passed_along(to_right, "dom", 1)
    from_right = passed_along(to_left, "dom", -1)
    mat_size = lax.axis_size("mat")
    up = [(i, (i + 1) % mat_size) for i in range(mat_size)]
    down = [(j, i) for i, j in up]
    row_above = lax.ppermute(masked[:, :, second_cells - 1], "mat", up)
    row_below = lax.ppermute(masked[:, :, 0], "mat", down)
    rows_right = jnp.stack(
        [row_above[:, upper_start - 1 : window_cells - 1], row_below[:, upper_start - 1 : window_cells - 1]]
    )
    rows_left = jnp.stack([row_above[:, 1 : patch_cells + 1], row_below[:, 1 : patch_cells + 1]])
    rows_from_left = passed_along(rows_right, "dom", 1)
    rows_from_right = passed_along(rows_left, "dom", -1)

    def with_rows(planes, rows):
        return jnp.concatenate([rows[0][:, :, None], planes, rows[1][:, :, None]], axis=2)

    zero_plane = jnp.zeros_like(masked[:, :1])
    zero_rows = jnp.zeros((2, block_orbs, 1, third_cells), masked.dtype)
    own_ext = with_rows(
        masked[:, patch_cells - 1 : upper_start + 1],
        jnp.stack([row_above[:, patch_cells - 1 : upper_start + 1], row_below[:, patch_cells - 1 : upper_start + 1]]),
    )
    left_ext = with_rows(
        jnp.concatenate([from_left, zero_plane, zero_plane], axis=1),
        jnp.concatenate([rows_from_left, zero_rows, zero_rows], axis=2),
    )
    right_ext = with_rows(
        jnp.concatenate([zero_plane, zero_plane, from_right], axis=1),
        jnp.concatenate([zero_rows, zero_rows, rows_from_right], axis=2),
    )
    phi_slots = [
        jnp.concatenate([from_left[:, 1:], zero_plane], axis=1),
        masked[:, patch_cells:upper_start],
        jnp.concatenate([zero_plane, from_right[:, :-1]], axis=1),
    ]
    applied_slots = [
        stencil(ext, potential).astype(jnp.bfloat16) for ext in (left_ext, own_ext, right_ext)
    ]
    full = jnp.stack(
        [
            jnp.stack(
                [
                    jnp.stack([pair_product(phi_slots[a], phi_slots[b]) for a in range(3)]),
                    jnp.stack([pair_product(applied_slots[a], phi_slots[b]) for a in range(3)]),
                ]
            )
            for b in range(3)
        ]
    )
    col_count = block_orbs // mat_count
    gram_rows, energy_rows = exchange_and_sum(full)
    columns = lax.axis_index("mat") * col_count + lax.iota(jnp.int32, col_count)
    block_ids = lax.iota(jnp.int32, local_blocks)
    column_pick = ((columns // per_block)[:, None] == block_ids[None, :]).astype(jnp.float32)
    row_pick = (
        (lax.iota(jnp.int32, block_orbs) // per_block)[:, None] == block_ids[None, :]
    ).astype(jnp.float32)
    select = jnp.einsum(
        "rkb,cb,ar->kca", correlation_pairs.astype(jnp.float32), column_pick, row_pick
    )
    return (gram_rows * select, energy_rows * select)


def solution(mesh):
    return jax.shard_map(
        on_device,
        mesh=mesh,
        in_specs=(
            P("dom", None, "mat", None),
            P("dom", "mat", None),
            P("dom"),
            P("dom"),
            P("dom"),
            P("dom", None, None),
        ),
        out_specs=(P(None, "mat", "dom"), P(None, "mat", "dom")),
        check_vma=False,
    )
```

```python
import jax
import jax.numpy as jnp
from jax import lax
from jax.sharding import PartitionSpec as P
from jax.experimental import pallas as pl
from jax.experimental.pallas import tpu as pltpu
import functools


def extended_2(array, sides, width):
    for axis, dim in sides:
        size, length = (lax.axis_size(axis), array.shape[dim])
        up = [(i, (i + 1) % size) for i in range(size)]
        down = [(j, i) for i, j in up]
        last = lax.slice_in_dim(array, length - width, length, axis=dim)
        first = lax.slice_in_dim(array, 0, width, axis=dim)
        before = lax.ppermute(last, axis, up)
        after = lax.ppermute(first, axis, down)
        array = jnp.concatenate([before, array, after], axis=dim)
    return array


def passed_along(block, axis, distance):
    devices = range(lax.axis_size(axis))
    route = [((i - distance) % len(devices), i) for i in devices]
    return lax.ppermute(block, axis, route)


def sphere_mask(
    centre_first,
    centre_second,
    centre_third,
    window_cells,
    patch_cells,
    second_cells,
    second_start,
    second_total,
    third_cells,
):
    planes = lax.iota(jnp.int32, window_cells)
    off_first = planes[None, :] - (patch_cells + centre_first[:, None])
    interior = (planes >= 1) & (planes <= window_cells - 2)
    second_coord = second_start + lax.iota(jnp.int32, second_cells)
    off_second = jnp.mod(second_coord[None, :] - centre_second[:, None], second_total)
    off_second = jnp.minimum(off_second, second_total - off_second)
    off_third = lax.iota(jnp.int32, third_cells)[None, :] - centre_third[:, None]
    radius = window_cells // 2
    distance = (
        (off_first * off_first)[:, :, None, None]
        + (off_second * off_second)[:, None, :, None]
        + (off_third * off_third)[:, None, None, :]
    )
    return (distance <= radius * radius) & interior[None, :, None, None]


def stencil(extended, potential_slab):
    centre_cells = extended[:, 1:-1, 1:-1, :].astype(jnp.float32)
    beside = extended[:, 2:, 1:-1, :].astype(jnp.float32) + extended[:, :-2, 1:-1, :].astype(
        jnp.float32
    )
    beside = (
        beside
        + extended[:, 1:-1, 2:, :].astype(jnp.float32)
        + extended[:, 1:-1, :-2, :].astype(jnp.float32)
    )
    third_padded = jnp.pad(centre_cells, ((0, 0), (0, 0), (0, 0), (1, 1)))
    beside = beside + third_padded[..., 2:] + third_padded[..., :-2]
    return 0.5 * (6.0 * centre_cells - beside) + potential_slab[None] * centre_cells


def pair_product(left, right):
    return lax.dot_general(
        left, right, (((1, 2, 3), (1, 2, 3)), ((), ())), preferred_element_type=jnp.float32
    )


def ring_scatter(full, axis):
    count = lax.axis_size("mat")
    me = lax.axis_index("mat")
    share = full.shape[axis] // count
    split = full.shape[-1] // 2
    halves = (full[..., :split], full[..., split:])
    forward = [(i, (i + 1) % count) for i in range(count)]
    backward = [((i + 1) % count, i) for i in range(count)]

    def chunk(values, index):
        return lax.dynamic_slice_in_dim(values, index * share, share, axis=axis)

    ahead = chunk(halves[0], lax.rem(me + count - 1, count))
    behind = chunk(halves[1], lax.rem(me + 1, count))
    for step in range(count - 1):
        ahead = lax.ppermute(ahead, "mat", forward)
        behind = lax.ppermute(behind, "mat", backward)
        ahead = ahead + chunk(halves[0], lax.rem(me + 2 * count - 2 - step, count))
        behind = behind + chunk(halves[1], lax.rem(me + 2 + step, count))
    return jnp.concatenate([ahead, behind], axis=-1)


def exchange_kernel(
    count, domains, share, half, x_ref, o_ref, total, from_left, from_right, stage_f, stage_b,
    land_f, land_b, dom_send, dom_recv, send_f, recv_f, send_b, recv_b,
):
    me = lax.axis_index("mat")
    dom = lax.axis_index("dom")
    right = lax.rem(me + 1, count)
    left = lax.rem(me + count - 1, count)
    up = lax.rem(dom + 1, domains)
    down = lax.rem(dom + domains - 1, domains)
    mesh_ids = pl.DeviceIdType.MESH
    barrier = pltpu.get_barrier_semaphore()
    for device in ((dom, left), (dom, right), (down, me), (up, me)):
        pl.semaphore_signal(barrier, 1, device_id=device, device_id_type=mesh_ids)
    pl.semaphore_wait(barrier, 4)

    exchanges = []
    for part in range(2):
        low = part * half
        to_down = pltpu.make_async_remote_copy(
            src_ref=x_ref.at[0, :, :, :, pl.ds(low, half)],
            dst_ref=from_right.at[part],
            send_sem=dom_send.at[2 * part],
            recv_sem=dom_recv.at[2 * part],
            device_id=(down, me),
            device_id_type=mesh_ids,
        )
        to_up = pltpu.make_async_remote_copy(
            src_ref=x_ref.at[2, :, :, :, pl.ds(low, half)],
            dst_ref=from_left.at[part],
            send_sem=dom_send.at[2 * part + 1],
            recv_sem=dom_recv.at[2 * part + 1],
            device_id=(up, me),
            device_id_type=mesh_ids,
        )
        to_down.start()
        to_up.start()
        exchanges.append((to_down, to_up))

    for part in range(2):
        low = part * half
        for copy in exchanges[part]:
            copy.wait()
        lefts, rights = from_left.at[part], from_right.at[part]
        here = total.at[part]
        here[:, 0] = lefts[:, 0]
        here[:, 1] = lefts[:, 1] + x_ref[1, :, 0, :, pl.ds(low, half)]
        here[:, 2] = lefts[:, 2] + x_ref[1, :, 1, :, pl.ds(low, half)] + rights[:, 0]
        here[:, 3] = x_ref[1, :, 2, :, pl.ds(low, half)] + rights[:, 1]
        here[:, 4] = rights[:, 2]

        def own(output, index):
            start = pl.multiple_of(index * share, share)
            return here[output, :, pl.ds(start, share), :]

        stage_f[part, 0] = own(0, lax.rem(me + count - 1, count))
        stage_b[part, 0] = own(1, lax.rem(me + 1, count))
        for step in range(count - 1):
            slot = part * (count - 1) + step
            ahead = pltpu.make_async_remote_copy(
                src_ref=stage_f.at[part, step],
                dst_ref=land_f.at[part, step],
                send_sem=send_f.at[slot],
                recv_sem=recv_f.at[slot],
                device_id=(dom, right),
                device_id_type=mesh_ids,
            )
            behind = pltpu.make_async_remote_copy(
                src_ref=stage_b.at[part, step],
                dst_ref=land_b.at[part, step],
                send_sem=send_b.at[slot],
                recv_sem=recv_b.at[slot],
                device_id=(dom, left),
                device_id_type=mesh_ids,
            )
            ahead.start()
            behind.start()
            ahead.wait()
            behind.wait()
            forward_sum = land_f[part, step] + own(0, lax.rem(me + 2 * count - 2 - step, count))
            backward_sum = land_b[part, step] + own(1, lax.rem(me + 2 + step, count))
            if step < count - 2:
                stage_f[part, step + 1] = forward_sum
                stage_b[part, step + 1] = backward_sum
            else:
                o_ref[0, :, :, pl.ds(low, half)] = forward_sum
                o_ref[1, :, :, pl.ds(low, half)] = backward_sum


def exchange_and_sum(full):
    count = lax.axis_size("mat")
    domains = lax.axis_size("dom")
    slots, outputs, columns, rows, cols = full.shape
    share = rows // count
    half = cols // 2
    offsets = 2 * columns - 1
    piece = pltpu.VMEM((2, count - 1, offsets, share, half), jnp.float32)
    arrived = pltpu.VMEM((2, outputs, columns, rows, half), jnp.float32)
    return pl.pallas_call(
        functools.partial(exchange_kernel, count, domains, share, half),
        out_shape=jax.ShapeDtypeStruct((outputs, offsets, share, cols), jnp.float32),
        in_specs=[pl.BlockSpec(memory_space=pltpu.VMEM)],
        out_specs=pl.BlockSpec(memory_space=pltpu.VMEM),
        scratch_shapes=[
            pltpu.VMEM((2, outputs, offsets, rows, half), jnp.float32),
            arrived,
            arrived,
            piece,
            piece,
            piece,
            piece,
        ]
        + [pltpu.SemaphoreType.DMA((4,))] * 2
        + [pltpu.SemaphoreType.DMA((2 * (count - 1),))] * 4,
        compiler_params=pltpu.CompilerParams(
            collective_id=0, has_side_effects=True, vmem_limit_bytes=48 * 1024 * 1024
        ),
    )(full)


def swap_kernel(domains, up_piece, down_piece, from_left, from_right, landed, send_sems, recv_sems):
    me = lax.axis_index("mat")
    dom = lax.axis_index("dom")
    up = lax.rem(dom + 1, domains)
    down = lax.rem(dom + domains - 1, domains)
    mesh_ids = pl.DeviceIdType.MESH
    barrier = pltpu.get_barrier_semaphore()
    for device in ((down, me), (up, me)):
        pl.semaphore_signal(barrier, 1, device_id=device, device_id_type=mesh_ids)
    pl.semaphore_wait(barrier, 2)
    copies = []
    for index, (source, target) in enumerate(((up_piece, up), (down_piece, down))):
        copy = pltpu.make_async_remote_copy(
            src_ref=source,
            dst_ref=landed.at[index],
            send_sem=send_sems.at[index],
            recv_sem=recv_sems.at[index],
            device_id=(target, me),
            device_id_type=mesh_ids,
        )
        copy.start()
        copies.append(copy)
    for copy in copies:
        copy.wait()
    from_left[...] = landed[0]
    from_right[...] = landed[1]


def swap_pieces(up_piece, down_piece):
    domains = lax.axis_size("dom")
    piece = jax.ShapeDtypeStruct(up_piece.shape, up_piece.dtype)
    return pl.pallas_call(
        functools.partial(swap_kernel, domains),
        out_shape=(piece, piece),
        in_specs=[pl.BlockSpec(memory_space=pltpu.VMEM)] * 2,
        out_specs=(pl.BlockSpec(memory_space=pltpu.VMEM),) * 2,
        scratch_shapes=[
            pltpu.VMEM((2,) + up_piece.shape, up_piece.dtype),
            pltpu.SemaphoreType.DMA((2,)),
            pltpu.SemaphoreType.DMA((2,)),
        ],
        compiler_params=pltpu.CompilerParams(
            collective_id=1, has_side_effects=True, vmem_limit_bytes=48 * 1024 * 1024
        ),
    )(up_piece, down_piece)


def on_device(orbitals, potential, centre_first, centre_second, centre_third, correlation_pairs):
    block_orbs, window_cells, second_cells, third_cells = orbitals.shape
    patch_cells = potential.shape[0]
    local_blocks = correlation_pairs.shape[0]
    per_block = block_orbs // local_blocks
    mat_count = lax.axis_size("mat")
    second_start = lax.axis_index("mat") * second_cells
    inside = sphere_mask(
        centre_first,
        centre_second,
        centre_third,
        window_cells,
        patch_cells,
        second_cells,
        second_start,
        second_cells * mat_count,
        third_cells,
    )
    masked = jnp.where(inside, orbitals, jnp.zeros_like(orbitals))
    upper_start = 2 * patch_cells
    to_right = masked[:, upper_start - 1 : window_cells - 1]
    to_left = masked[:, 1 : patch_cells + 1]
    from_left, from_right = swap_pieces(to_right, to_left)
    mat_size = lax.axis_size("mat")
    up = [(i, (i + 1) % mat_size) for i in range(mat_size)]
    down = [(j, i) for i, j in up]
    row_above = lax.ppermute(masked[:, :, second_cells - 1], "mat", up)
    row_below = lax.ppermute(masked[:, :, 0], "mat", down)
    rows_right = jnp.stack(
        [row_above[:, upper_start - 1 : window_cells - 1], row_below[:, upper_start - 1 : window_cells - 1]]
    )
    rows_left = jnp.stack([row_above[:, 1 : patch_cells + 1], row_below[:, 1 : patch_cells + 1]])
    rows_from_left = passed_along(rows_right, "dom", 1)
    rows_from_right = passed_along(rows_left, "dom", -1)

    def with_rows(planes, rows):
        return jnp.concatenate([rows[0][:, :, None], planes, rows[1][:, :, None]], axis=2)

    zero_plane = jnp.zeros_like(masked[:, :1])
    zero_rows = jnp.zeros((2, block_orbs, 1, third_cells), masked.dtype)
    own_ext = with_rows(
        masked[:, patch_cells - 1 : upper_start + 1],
        jnp.stack([row_above[:, patch_cells - 1 : upper_start + 1], row_below[:, patch_cells - 1 : upper_start + 1]]),
    )
    left_ext = with_rows(
        jnp.concatenate([from_left, zero_plane, zero_plane], axis=1),
        jnp.concatenate([rows_from_left, zero_rows, zero_rows], axis=2),
    )
    right_ext = with_rows(
        jnp.concatenate([zero_plane, zero_plane, from_right], axis=1),
        jnp.concatenate([zero_rows, zero_rows, rows_from_right], axis=2),
    )
    phi_slots = [
        jnp.concatenate([from_left[:, 1:], zero_plane], axis=1),
        masked[:, patch_cells:upper_start],
        jnp.concatenate([zero_plane, from_right[:, :-1]], axis=1),
    ]
    applied_slots = [
        stencil(ext, potential).astype(jnp.bfloat16) for ext in (left_ext, own_ext, right_ext)
    ]
    full = jnp.stack(
        [
            jnp.stack(
                [
                    jnp.stack([pair_product(phi_slots[a], phi_slots[b]) for a in range(3)]),
                    jnp.stack([pair_product(applied_slots[a], phi_slots[b]) for a in range(3)]),
                ]
            )
            for b in range(3)
        ]
    )
    col_count = block_orbs // mat_count
    gram_rows, energy_rows = exchange_and_sum(full)
    columns = lax.axis_index("mat") * col_count + lax.iota(jnp.int32, col_count)
    block_ids = lax.iota(jnp.int32, local_blocks)
    column_pick = ((columns // per_block)[:, None] == block_ids[None, :]).astype(jnp.float32)
    row_pick = (
        (lax.iota(jnp.int32, block_orbs) // per_block)[:, None] == block_ids[None, :]
    ).astype(jnp.float32)
    select = jnp.einsum(
        "rkb,cb,ar->kca", correlation_pairs.astype(jnp.float32), column_pick, row_pick
    )
    return (gram_rows * select, energy_rows * select)


def solution(mesh):
    return jax.shard_map(
        on_device,
        mesh=mesh,
        in_specs=(
            P("dom", None, "mat", None),
            P("dom", "mat", None),
            P("dom"),
            P("dom"),
            P("dom"),
            P("dom", None, None),
        ),
        out_specs=(P(None, "mat", "dom"), P(None, "mat", "dom")),
        check_vma=False,
    )
```

```python
import jax
import jax.numpy as jnp
from jax import lax
from jax.sharding import PartitionSpec as P
from jax.experimental import pallas as pl
from jax.experimental.pallas import tpu as pltpu
import functools


def extended_2(array, sides, width):
    for axis, dim in sides:
        size, length = (lax.axis_size(axis), array.shape[dim])
        up = [(i, (i + 1) % size) for i in range(size)]
        down = [(j, i) for i, j in up]
        last = lax.slice_in_dim(array, length - width, length, axis=dim)
        first = lax.slice_in_dim(array, 0, width, axis=dim)
        before = lax.ppermute(last, axis, up)
        after = lax.ppermute(first, axis, down)
        array = jnp.concatenate([before, array, after], axis=dim)
    return array


def passed_along(block, axis, distance):
    devices = range(lax.axis_size(axis))
    route = [((i - distance) % len(devices), i) for i in devices]
    return lax.ppermute(block, axis, route)


def sphere_mask(
    centre_first,
    centre_second,
    centre_third,
    window_cells,
    patch_cells,
    second_cells,
    second_start,
    second_total,
    third_cells,
):
    planes = lax.iota(jnp.int32, window_cells)
    off_first = planes[None, :] - (patch_cells + centre_first[:, None])
    interior = (planes >= 1) & (planes <= window_cells - 2)
    second_coord = second_start + lax.iota(jnp.int32, second_cells)
    off_second = jnp.mod(second_coord[None, :] - centre_second[:, None], second_total)
    off_second = jnp.minimum(off_second, second_total - off_second)
    off_third = lax.iota(jnp.int32, third_cells)[None, :] - centre_third[:, None]
    radius = window_cells // 2
    distance = (
        (off_first * off_first)[:, :, None, None]
        + (off_second * off_second)[:, None, :, None]
        + (off_third * off_third)[:, None, None, :]
    )
    return (distance <= radius * radius) & interior[None, :, None, None]


def stencil(extended, potential_slab):
    centre_cells = extended[:, 1:-1, 1:-1, :].astype(jnp.float32)
    beside = extended[:, 2:, 1:-1, :].astype(jnp.float32) + extended[:, :-2, 1:-1, :].astype(
        jnp.float32
    )
    beside = (
        beside
        + extended[:, 1:-1, 2:, :].astype(jnp.float32)
        + extended[:, 1:-1, :-2, :].astype(jnp.float32)
    )
    third_padded = jnp.pad(centre_cells, ((0, 0), (0, 0), (0, 0), (1, 1)))
    beside = beside + third_padded[..., 2:] + third_padded[..., :-2]
    return 0.5 * (6.0 * centre_cells - beside) + potential_slab[None] * centre_cells


def pair_product(left, right):
    return lax.dot_general(
        left, right, (((1, 2, 3), (1, 2, 3)), ((), ())), preferred_element_type=jnp.float32
    )


def ring_scatter(full, axis):
    count = lax.axis_size("mat")
    me = lax.axis_index("mat")
    share = full.shape[axis] // count
    split = full.shape[-1] // 2
    halves = (full[..., :split], full[..., split:])
    forward = [(i, (i + 1) % count) for i in range(count)]
    backward = [((i + 1) % count, i) for i in range(count)]

    def chunk(values, index):
        return lax.dynamic_slice_in_dim(values, index * share, share, axis=axis)

    ahead = chunk(halves[0], lax.rem(me + count - 1, count))
    behind = chunk(halves[1], lax.rem(me + 1, count))
    for step in range(count - 1):
        ahead = lax.ppermute(ahead, "mat", forward)
        behind = lax.ppermute(behind, "mat", backward)
        ahead = ahead + chunk(halves[0], lax.rem(me + 2 * count - 2 - step, count))
        behind = behind + chunk(halves[1], lax.rem(me + 2 + step, count))
    return jnp.concatenate([ahead, behind], axis=-1)


def exchange_kernel(
    count, domains, share, half, x_ref, o_ref, total, from_left, from_right, stage_f, stage_b,
    land_f, land_b, dom_send, dom_recv, send_f, recv_f, send_b, recv_b,
):
    me = lax.axis_index("mat")
    dom = lax.axis_index("dom")
    right = lax.rem(me + 1, count)
    left = lax.rem(me + count - 1, count)
    up = lax.rem(dom + 1, domains)
    down = lax.rem(dom + domains - 1, domains)
    mesh_ids = pl.DeviceIdType.MESH
    barrier = pltpu.get_barrier_semaphore()
    for device in ((dom, left), (dom, right), (down, me), (up, me)):
        pl.semaphore_signal(barrier, 1, device_id=device, device_id_type=mesh_ids)
    pl.semaphore_wait(barrier, 4)

    exchanges = []
    for part in range(2):
        low = part * half
        to_down = pltpu.make_async_remote_copy(
            src_ref=x_ref.at[0, :, :, :, pl.ds(low, half)],
            dst_ref=from_right.at[part],
            send_sem=dom_send.at[2 * part],
            recv_sem=dom_recv.at[2 * part],
            device_id=(down, me),
            device_id_type=mesh_ids,
        )
        to_up = pltpu.make_async_remote_copy(
            src_ref=x_ref.at[2, :, :, :, pl.ds(low, half)],
            dst_ref=from_left.at[part],
            send_sem=dom_send.at[2 * part + 1],
            recv_sem=dom_recv.at[2 * part + 1],
            device_id=(up, me),
            device_id_type=mesh_ids,
        )
        to_down.start()
        to_up.start()
        exchanges.append((to_down, to_up))

    for part in range(2):
        low = part * half
        for copy in exchanges[part]:
            copy.wait()
        lefts, rights = from_left.at[part], from_right.at[part]
        here = total.at[part]
        here[:, 0] = lefts[:, 0]
        here[:, 1] = lefts[:, 1] + x_ref[1, :, 0, :, pl.ds(low, half)]
        here[:, 2] = lefts[:, 2] + x_ref[1, :, 1, :, pl.ds(low, half)] + rights[:, 0]
        here[:, 3] = x_ref[1, :, 2, :, pl.ds(low, half)] + rights[:, 1]
        here[:, 4] = rights[:, 2]

        def own(output, index):
            start = pl.multiple_of(index * share, share)
            return here[output, :, pl.ds(start, share), :]

        stage_f[part, 0] = own(0, lax.rem(me + count - 1, count))
        stage_b[part, 0] = own(1, lax.rem(me + 1, count))
        for step in range(count - 1):
            slot = part * (count - 1) + step
            ahead = pltpu.make_async_remote_copy(
                src_ref=stage_f.at[part, step],
                dst_ref=land_f.at[part, step],
                send_sem=send_f.at[slot],
                recv_sem=recv_f.at[slot],
                device_id=(dom, right),
                device_id_type=mesh_ids,
            )
            behind = pltpu.make_async_remote_copy(
                src_ref=stage_b.at[part, step],
                dst_ref=land_b.at[part, step],
                send_sem=send_b.at[slot],
                recv_sem=recv_b.at[slot],
                device_id=(dom, left),
                device_id_type=mesh_ids,
            )
            ahead.start()
            behind.start()
            ahead.wait()
            behind.wait()
            forward_sum = land_f[part, step] + own(0, lax.rem(me + 2 * count - 2 - step, count))
            backward_sum = land_b[part, step] + own(1, lax.rem(me + 2 + step, count))
            if step < count - 2:
                stage_f[part, step + 1] = forward_sum
                stage_b[part, step + 1] = backward_sum
            else:
                o_ref[0, :, :, pl.ds(low, half)] = forward_sum
                o_ref[1, :, :, pl.ds(low, half)] = backward_sum


def exchange_and_sum(full):
    count = lax.axis_size("mat")
    domains = lax.axis_size("dom")
    slots, outputs, columns, rows, cols = full.shape
    share = rows // count
    half = cols // 2
    offsets = 2 * columns - 1
    piece = pltpu.VMEM((2, count - 1, offsets, share, half), jnp.float32)
    arrived = pltpu.VMEM((2, outputs, columns, rows, half), jnp.float32)
    return pl.pallas_call(
        functools.partial(exchange_kernel, count, domains, share, half),
        out_shape=jax.ShapeDtypeStruct((outputs, offsets, share, cols), jnp.float32),
        in_specs=[pl.BlockSpec(memory_space=pltpu.VMEM)],
        out_specs=pl.BlockSpec(memory_space=pltpu.VMEM),
        scratch_shapes=[
            pltpu.VMEM((2, outputs, offsets, rows, half), jnp.float32),
            arrived,
            arrived,
            piece,
            piece,
            piece,
            piece,
        ]
        + [pltpu.SemaphoreType.DMA((4,))] * 2
        + [pltpu.SemaphoreType.DMA((2 * (count - 1),))] * 4,
        compiler_params=pltpu.CompilerParams(
            collective_id=0, has_side_effects=True, vmem_limit_bytes=48 * 1024 * 1024
        ),
    )(full)


def on_device(orbitals, potential, centre_first, centre_second, centre_third, correlation_pairs):
    block_orbs, window_cells, second_cells, third_cells = orbitals.shape
    patch_cells = potential.shape[0]
    local_blocks = correlation_pairs.shape[0]
    per_block = block_orbs // local_blocks
    mat_count = lax.axis_size("mat")
    second_start = lax.axis_index("mat") * second_cells
    inside = sphere_mask(
        centre_first,
        centre_second,
        centre_third,
        window_cells,
        patch_cells,
        second_cells,
        second_start,
        second_cells * mat_count,
        third_cells,
    )
    masked = jnp.where(inside, orbitals, jnp.zeros_like(orbitals))
    upper_start = 2 * patch_cells
    to_right = masked[:, upper_start - 1 : window_cells - 1]
    to_left = masked[:, 1 : patch_cells + 1]
    from_left = passed_along(to_right, "dom", 1)
    from_right = passed_along(to_left, "dom", -1)
    mat_size = lax.axis_size("mat")
    up = [(i, (i + 1) % mat_size) for i in range(mat_size)]
    down = [(j, i) for i, j in up]
    row_above = lax.ppermute(masked[:, :, second_cells - 1], "mat", up)
    row_below = lax.ppermute(masked[:, :, 0], "mat", down)
    arrived = jnp.stack([from_left, from_right])
    arrived_above = lax.ppermute(arrived[:, :, :, second_cells - 1], "mat", up)
    arrived_below = lax.ppermute(arrived[:, :, :, 0], "mat", down)
    rows_from_left = jnp.stack([arrived_above[0], arrived_below[0]])
    rows_from_right = jnp.stack([arrived_above[1], arrived_below[1]])

    def with_rows(planes, rows):
        return jnp.concatenate([rows[0][:, :, None], planes, rows[1][:, :, None]], axis=2)

    zero_plane = jnp.zeros_like(masked[:, :1])
    zero_rows = jnp.zeros((2, block_orbs, 1, third_cells), masked.dtype)
    own_ext = with_rows(
        masked[:, patch_cells - 1 : upper_start + 1],
        jnp.stack([row_above[:, patch_cells - 1 : upper_start + 1], row_below[:, patch_cells - 1 : upper_start + 1]]),
    )
    left_ext = with_rows(
        jnp.concatenate([from_left, zero_plane, zero_plane], axis=1),
        jnp.concatenate([rows_from_left, zero_rows, zero_rows], axis=2),
    )
    right_ext = with_rows(
        jnp.concatenate([zero_plane, zero_plane, from_right], axis=1),
        jnp.concatenate([zero_rows, zero_rows, rows_from_right], axis=2),
    )
    phi_slots = [
        jnp.concatenate([from_left[:, 1:], zero_plane], axis=1),
        masked[:, patch_cells:upper_start],
        jnp.concatenate([zero_plane, from_right[:, :-1]], axis=1),
    ]
    applied_slots = [
        stencil(ext, potential).astype(jnp.bfloat16) for ext in (left_ext, own_ext, right_ext)
    ]
    full = jnp.stack(
        [
            jnp.stack(
                [
                    jnp.stack([pair_product(phi_slots[a], phi_slots[b]) for a in range(3)]),
                    jnp.stack([pair_product(applied_slots[a], phi_slots[b]) for a in range(3)]),
                ]
            )
            for b in range(3)
        ]
    )
    col_count = block_orbs // mat_count
    gram_rows, energy_rows = exchange_and_sum(full)
    columns = lax.axis_index("mat") * col_count + lax.iota(jnp.int32, col_count)
    block_ids = lax.iota(jnp.int32, local_blocks)
    column_pick = ((columns // per_block)[:, None] == block_ids[None, :]).astype(jnp.float32)
    row_pick = (
        (lax.iota(jnp.int32, block_orbs) // per_block)[:, None] == block_ids[None, :]
    ).astype(jnp.float32)
    select = jnp.einsum(
        "rkb,cb,ar->kca", correlation_pairs.astype(jnp.float32), column_pick, row_pick
    )
    return (gram_rows * select, energy_rows * select)


def solution(mesh):
    return jax.shard_map(
        on_device,
        mesh=mesh,
        in_specs=(
            P("dom", None, "mat", None),
            P("dom", "mat", None),
            P("dom"),
            P("dom"),
            P("dom"),
            P("dom", None, None),
        ),
        out_specs=(P(None, "mat", "dom"), P(None, "mat", "dom")),
        check_vma=False,
    )
```

```python
import jax
import jax.numpy as jnp
from jax import lax
from jax.sharding import PartitionSpec as P
from jax.experimental import pallas as pl
from jax.experimental.pallas import tpu as pltpu
import functools


def extended_2(array, sides, width):
    for axis, dim in sides:
        size, length = (lax.axis_size(axis), array.shape[dim])
        up = [(i, (i + 1) % size) for i in range(size)]
        down = [(j, i) for i, j in up]
        last = lax.slice_in_dim(array, length - width, length, axis=dim)
        first = lax.slice_in_dim(array, 0, width, axis=dim)
        before = lax.ppermute(last, axis, up)
        after = lax.ppermute(first, axis, down)
        array = jnp.concatenate([before, array, after], axis=dim)
    return array


def passed_along(block, axis, distance):
    devices = range(lax.axis_size(axis))
    route = [((i - distance) % len(devices), i) for i in devices]
    return lax.ppermute(block, axis, route)


def sphere_mask(
    centre_first,
    centre_second,
    centre_third,
    window_cells,
    patch_cells,
    second_cells,
    second_start,
    second_total,
    third_cells,
):
    planes = lax.iota(jnp.int32, window_cells)
    off_first = planes[None, :] - (patch_cells + centre_first[:, None])
    interior = (planes >= 1) & (planes <= window_cells - 2)
    second_coord = second_start + lax.iota(jnp.int32, second_cells)
    off_second = jnp.mod(second_coord[None, :] - centre_second[:, None], second_total)
    off_second = jnp.minimum(off_second, second_total - off_second)
    off_third = lax.iota(jnp.int32, third_cells)[None, :] - centre_third[:, None]
    radius = window_cells // 2
    distance = (
        (off_first * off_first)[:, :, None, None]
        + (off_second * off_second)[:, None, :, None]
        + (off_third * off_third)[:, None, None, :]
    )
    return (distance <= radius * radius) & interior[None, :, None, None]


def stencil(extended, potential_slab):
    centre_cells = extended[:, 1:-1, 1:-1, :].astype(jnp.float32)
    beside = extended[:, 2:, 1:-1, :].astype(jnp.float32) + extended[:, :-2, 1:-1, :].astype(
        jnp.float32
    )
    beside = (
        beside
        + extended[:, 1:-1, 2:, :].astype(jnp.float32)
        + extended[:, 1:-1, :-2, :].astype(jnp.float32)
    )
    third_padded = jnp.pad(centre_cells, ((0, 0), (0, 0), (0, 0), (1, 1)))
    beside = beside + third_padded[..., 2:] + third_padded[..., :-2]
    return 0.5 * (6.0 * centre_cells - beside) + potential_slab[None] * centre_cells


def pair_product(left, right):
    return lax.dot_general(
        left, right, (((1, 2, 3), (1, 2, 3)), ((), ())), preferred_element_type=jnp.float32
    )


def ring_scatter(full, axis):
    count = lax.axis_size("mat")
    me = lax.axis_index("mat")
    share = full.shape[axis] // count
    split = full.shape[-1] // 2
    halves = (full[..., :split], full[..., split:])
    forward = [(i, (i + 1) % count) for i in range(count)]
    backward = [((i + 1) % count, i) for i in range(count)]

    def chunk(values, index):
        return lax.dynamic_slice_in_dim(values, index * share, share, axis=axis)

    ahead = chunk(halves[0], lax.rem(me + count - 1, count))
    behind = chunk(halves[1], lax.rem(me + 1, count))
    for step in range(count - 1):
        ahead = lax.ppermute(ahead, "mat", forward)
        behind = lax.ppermute(behind, "mat", backward)
        ahead = ahead + chunk(halves[0], lax.rem(me + 2 * count - 2 - step, count))
        behind = behind + chunk(halves[1], lax.rem(me + 2 + step, count))
    return jnp.concatenate([ahead, behind], axis=-1)


def exchange_kernel(
    count, domains, share, half, x_ref, o_ref, total, from_left, from_right, stage_f, stage_b,
    land_f, land_b, dom_send, dom_recv, send_f, recv_f, send_b, recv_b,
):
    me = lax.axis_index("mat")
    dom = lax.axis_index("dom")
    right = lax.rem(me + 1, count)
    left = lax.rem(me + count - 1, count)
    up = lax.rem(dom + 1, domains)
    down = lax.rem(dom + domains - 1, domains)
    mesh_ids = pl.DeviceIdType.MESH
    barrier = pltpu.get_barrier_semaphore()
    for device in ((dom, left), (dom, right), (down, me), (up, me)):
        pl.semaphore_signal(barrier, 1, device_id=device, device_id_type=mesh_ids)
    pl.semaphore_wait(barrier, 4)

    exchanges = []
    for part in range(2):
        low = part * half
        to_down = pltpu.make_async_remote_copy(
            src_ref=x_ref.at[0, :, :, :, pl.ds(low, half)],
            dst_ref=from_right.at[part],
            send_sem=dom_send.at[2 * part],
            recv_sem=dom_recv.at[2 * part],
            device_id=(down, me),
            device_id_type=mesh_ids,
        )
        to_up = pltpu.make_async_remote_copy(
            src_ref=x_ref.at[2, :, :, :, pl.ds(low, half)],
            dst_ref=from_left.at[part],
            send_sem=dom_send.at[2 * part + 1],
            recv_sem=dom_recv.at[2 * part + 1],
            device_id=(up, me),
            device_id_type=mesh_ids,
        )
        to_down.start()
        to_up.start()
        exchanges.append((to_down, to_up))

    for part in range(2):
        low = part * half
        for copy in exchanges[part]:
            copy.wait()
        lefts, rights = from_left.at[part], from_right.at[part]
        here = total.at[part]
        here[:, 0] = lefts[:, 0]
        here[:, 1] = lefts[:, 1] + x_ref[1, :, 0, :, pl.ds(low, half)]
        here[:, 2] = lefts[:, 2] + x_ref[1, :, 1, :, pl.ds(low, half)] + rights[:, 0]
        here[:, 3] = x_ref[1, :, 2, :, pl.ds(low, half)] + rights[:, 1]
        here[:, 4] = rights[:, 2]

        def own(output, index):
            start = pl.multiple_of(index * share, share)
            return here[output, :, pl.ds(start, share), :]

        stage_f[part, 0] = own(0, lax.rem(me + count - 1, count))
        stage_b[part, 0] = own(1, lax.rem(me + 1, count))
        for step in range(count - 1):
            slot = part * (count - 1) + step
            ahead = pltpu.make_async_remote_copy(
                src_ref=stage_f.at[part, step],
                dst_ref=land_f.at[part, step],
                send_sem=send_f.at[slot],
                recv_sem=recv_f.at[slot],
                device_id=(dom, right),
                device_id_type=mesh_ids,
            )
            behind = pltpu.make_async_remote_copy(
                src_ref=stage_b.at[part, step],
                dst_ref=land_b.at[part, step],
                send_sem=send_b.at[slot],
                recv_sem=recv_b.at[slot],
                device_id=(dom, left),
                device_id_type=mesh_ids,
            )
            ahead.start()
            behind.start()
            ahead.wait()
            behind.wait()
            forward_sum = land_f[part, step] + own(0, lax.rem(me + 2 * count - 2 - step, count))
            backward_sum = land_b[part, step] + own(1, lax.rem(me + 2 + step, count))
            if step < count - 2:
                stage_f[part, step + 1] = forward_sum
                stage_b[part, step + 1] = backward_sum
            else:
                o_ref[0, :, :, pl.ds(low, half)] = forward_sum
                o_ref[1, :, :, pl.ds(low, half)] = backward_sum


def exchange_and_sum(full):
    count = lax.axis_size("mat")
    domains = lax.axis_size("dom")
    slots, outputs, columns, rows, cols = full.shape
    share = rows // count
    half = cols // 2
    offsets = 2 * columns - 1
    piece = pltpu.VMEM((2, count - 1, offsets, share, half), jnp.float32)
    arrived = pltpu.VMEM((2, outputs, columns, rows, half), jnp.float32)
    return pl.pallas_call(
        functools.partial(exchange_kernel, count, domains, share, half),
        out_shape=jax.ShapeDtypeStruct((outputs, offsets, share, cols), jnp.float32),
        in_specs=[pl.BlockSpec(memory_space=pltpu.VMEM)],
        out_specs=pl.BlockSpec(memory_space=pltpu.VMEM),
        scratch_shapes=[
            pltpu.VMEM((2, outputs, offsets, rows, half), jnp.float32),
            arrived,
            arrived,
            piece,
            piece,
            piece,
            piece,
        ]
        + [pltpu.SemaphoreType.DMA((4,))] * 2
        + [pltpu.SemaphoreType.DMA((2 * (count - 1),))] * 4,
        compiler_params=pltpu.CompilerParams(
            collective_id=0, has_side_effects=True, vmem_limit_bytes=48 * 1024 * 1024
        ),
    )(full)


def on_device(orbitals, potential, centre_first, centre_second, centre_third, correlation_pairs):
    block_orbs, window_cells, second_cells, third_cells = orbitals.shape
    patch_cells = potential.shape[0]
    local_blocks = correlation_pairs.shape[0]
    per_block = block_orbs // local_blocks
    mat_count = lax.axis_size("mat")
    second_start = lax.axis_index("mat") * second_cells
    inside = sphere_mask(
        centre_first,
        centre_second,
        centre_third,
        window_cells,
        patch_cells,
        second_cells,
        second_start,
        second_cells * mat_count,
        third_cells,
    )
    masked = jnp.where(inside, orbitals, jnp.zeros_like(orbitals))
    upper_start = 2 * patch_cells
    to_right = masked[:, upper_start - 1 : window_cells - 1]
    to_left = masked[:, 1 : patch_cells + 1]
    from_left = passed_along(to_right, "dom", 1)
    from_right = passed_along(to_left, "dom", -1)
    mat_size = lax.axis_size("mat")
    up = [(i, (i + 1) % mat_size) for i in range(mat_size)]
    down = [(j, i) for i, j in up]
    own_planes = masked[:, patch_cells - 1 : upper_start + 1]
    row_above = lax.ppermute(own_planes[:, :, second_cells - 1], "mat", up)
    row_below = lax.ppermute(own_planes[:, :, 0], "mat", down)
    arrived = jnp.stack([from_left, from_right])
    arrived_above = lax.ppermute(arrived[:, :, :, second_cells - 1], "mat", up)
    arrived_below = lax.ppermute(arrived[:, :, :, 0], "mat", down)
    rows_from_left = jnp.stack([arrived_above[0], arrived_below[0]])
    rows_from_right = jnp.stack([arrived_above[1], arrived_below[1]])

    def with_rows(planes, rows):
        return jnp.concatenate([rows[0][:, :, None], planes, rows[1][:, :, None]], axis=2)

    zero_plane = jnp.zeros_like(masked[:, :1])
    zero_rows = jnp.zeros((2, block_orbs, 1, third_cells), masked.dtype)
    own_ext = with_rows(
        masked[:, patch_cells - 1 : upper_start + 1],
        jnp.stack([row_above, row_below]),
    )
    left_ext = with_rows(
        jnp.concatenate([from_left, zero_plane, zero_plane], axis=1),
        jnp.concatenate([rows_from_left, zero_rows, zero_rows], axis=2),
    )
    right_ext = with_rows(
        jnp.concatenate([zero_plane, zero_plane, from_right], axis=1),
        jnp.concatenate([zero_rows, zero_rows, rows_from_right], axis=2),
    )
    phi_slots = [
        jnp.concatenate([from_left[:, 1:], zero_plane], axis=1),
        masked[:, patch_cells:upper_start],
        jnp.concatenate([zero_plane, from_right[:, :-1]], axis=1),
    ]
    applied_slots = [
        stencil(ext, potential).astype(jnp.bfloat16) for ext in (left_ext, own_ext, right_ext)
    ]
    full = jnp.stack(
        [
            jnp.stack(
                [
                    jnp.stack([pair_product(phi_slots[a], phi_slots[b]) for a in range(3)]),
                    jnp.stack([pair_product(applied_slots[a], phi_slots[b]) for a in range(3)]),
                ]
            )
            for b in range(3)
        ]
    )
    col_count = block_orbs // mat_count
    gram_rows, energy_rows = exchange_and_sum(full)
    columns = lax.axis_index("mat") * col_count + lax.iota(jnp.int32, col_count)
    block_ids = lax.iota(jnp.int32, local_blocks)
    column_pick = ((columns // per_block)[:, None] == block_ids[None, :]).astype(jnp.float32)
    row_pick = (
        (lax.iota(jnp.int32, block_orbs) // per_block)[:, None] == block_ids[None, :]
    ).astype(jnp.float32)
    select = jnp.einsum(
        "rkb,cb,ar->kca", correlation_pairs.astype(jnp.float32), column_pick, row_pick
    )
    return (gram_rows * select, energy_rows * select)


def solution(mesh):
    return jax.shard_map(
        on_device,
        mesh=mesh,
        in_specs=(
            P("dom", None, "mat", None),
            P("dom", "mat", None),
            P("dom"),
            P("dom"),
            P("dom"),
            P("dom", None, None),
        ),
        out_specs=(P(None, "mat", "dom"), P(None, "mat", "dom")),
        check_vma=False,
    )
```

```python
import jax
import jax.numpy as jnp
from jax import lax
from jax.sharding import PartitionSpec as P
from jax.experimental import pallas as pl
from jax.experimental.pallas import tpu as pltpu
import functools


def extended_2(array, sides, width):
    for axis, dim in sides:
        size, length = (lax.axis_size(axis), array.shape[dim])
        up = [(i, (i + 1) % size) for i in range(size)]
        down = [(j, i) for i, j in up]
        last = lax.slice_in_dim(array, length - width, length, axis=dim)
        first = lax.slice_in_dim(array, 0, width, axis=dim)
        before = lax.ppermute(last, axis, up)
        after = lax.ppermute(first, axis, down)
        array = jnp.concatenate([before, array, after], axis=dim)
    return array


def passed_along(block, axis, distance):
    devices = range(lax.axis_size(axis))
    route = [((i - distance) % len(devices), i) for i in devices]
    return lax.ppermute(block, axis, route)


def sphere_mask(
    centre_first,
    centre_second,
    centre_third,
    window_cells,
    patch_cells,
    second_cells,
    second_start,
    second_total,
    third_cells,
):
    planes = lax.iota(jnp.int32, window_cells)
    off_first = planes[None, :] - (patch_cells + centre_first[:, None])
    interior = (planes >= 1) & (planes <= window_cells - 2)
    second_coord = second_start + lax.iota(jnp.int32, second_cells)
    off_second = jnp.mod(second_coord[None, :] - centre_second[:, None], second_total)
    off_second = jnp.minimum(off_second, second_total - off_second)
    off_third = lax.iota(jnp.int32, third_cells)[None, :] - centre_third[:, None]
    radius = window_cells // 2
    distance = (
        (off_first * off_first)[:, :, None, None]
        + (off_second * off_second)[:, None, :, None]
        + (off_third * off_third)[:, None, None, :]
    )
    return (distance <= radius * radius) & interior[None, :, None, None]


def stencil(extended, potential_slab):
    centre_cells = extended[:, 1:-1, 1:-1, :].astype(jnp.float32)
    beside = extended[:, 2:, 1:-1, :].astype(jnp.float32) + extended[:, :-2, 1:-1, :].astype(
        jnp.float32
    )
    beside = (
        beside
        + extended[:, 1:-1, 2:, :].astype(jnp.float32)
        + extended[:, 1:-1, :-2, :].astype(jnp.float32)
    )
    third_padded = jnp.pad(centre_cells, ((0, 0), (0, 0), (0, 0), (1, 1)))
    beside = beside + third_padded[..., 2:] + third_padded[..., :-2]
    return 0.5 * (6.0 * centre_cells - beside) + potential_slab[None] * centre_cells


def pair_product(left, right):
    return lax.dot_general(
        left, right, (((1, 2, 3), (1, 2, 3)), ((), ())), preferred_element_type=jnp.float32
    )


def ring_scatter(full, axis):
    count = lax.axis_size("mat")
    me = lax.axis_index("mat")
    share = full.shape[axis] // count
    split = full.shape[-1] // 2
    halves = (full[..., :split], full[..., split:])
    forward = [(i, (i + 1) % count) for i in range(count)]
    backward = [((i + 1) % count, i) for i in range(count)]

    def chunk(values, index):
        return lax.dynamic_slice_in_dim(values, index * share, share, axis=axis)

    ahead = chunk(halves[0], lax.rem(me + count - 1, count))
    behind = chunk(halves[1], lax.rem(me + 1, count))
    for step in range(count - 1):
        ahead = lax.ppermute(ahead, "mat", forward)
        behind = lax.ppermute(behind, "mat", backward)
        ahead = ahead + chunk(halves[0], lax.rem(me + 2 * count - 2 - step, count))
        behind = behind + chunk(halves[1], lax.rem(me + 2 + step, count))
    return jnp.concatenate([ahead, behind], axis=-1)


def exchange_kernel(
    count, domains, share, half, x_ref, o_ref, total, from_left, from_right, stage_f, stage_b,
    land_f, land_b, dom_send, dom_recv, send_f, recv_f, send_b, recv_b,
):
    me = lax.axis_index("mat")
    dom = lax.axis_index("dom")
    right = lax.rem(me + 1, count)
    left = lax.rem(me + count - 1, count)
    up = lax.rem(dom + 1, domains)
    down = lax.rem(dom + domains - 1, domains)
    mesh_ids = pl.DeviceIdType.MESH
    barrier = pltpu.get_barrier_semaphore()
    for device in ((dom, left), (dom, right), (down, me), (up, me)):
        pl.semaphore_signal(barrier, 1, device_id=device, device_id_type=mesh_ids)
    pl.semaphore_wait(barrier, 4)

    exchanges = []
    for part in range(2):
        low = part * half
        to_down = pltpu.make_async_remote_copy(
            src_ref=x_ref.at[0, :, :, :, pl.ds(low, half)],
            dst_ref=from_right.at[part],
            send_sem=dom_send.at[2 * part],
            recv_sem=dom_recv.at[2 * part],
            device_id=(down, me),
            device_id_type=mesh_ids,
        )
        to_up = pltpu.make_async_remote_copy(
            src_ref=x_ref.at[2, :, :, :, pl.ds(low, half)],
            dst_ref=from_left.at[part],
            send_sem=dom_send.at[2 * part + 1],
            recv_sem=dom_recv.at[2 * part + 1],
            device_id=(up, me),
            device_id_type=mesh_ids,
        )
        to_down.start()
        to_up.start()
        exchanges.append((to_down, to_up))

    for part in range(2):
        low = part * half
        for copy in exchanges[part]:
            copy.wait()
        lefts, rights = from_left.at[part], from_right.at[part]
        here = total.at[part]
        here[:, 0] = lefts[:, 0]
        here[:, 1] = lefts[:, 1] + x_ref[1, :, 0, :, pl.ds(low, half)]
        here[:, 2] = lefts[:, 2] + x_ref[1, :, 1, :, pl.ds(low, half)] + rights[:, 0]
        here[:, 3] = x_ref[1, :, 2, :, pl.ds(low, half)] + rights[:, 1]
        here[:, 4] = rights[:, 2]

        def own(output, index):
            start = pl.multiple_of(index * share, share)
            return here[output, :, pl.ds(start, share), :]

        stage_f[part, 0] = own(0, lax.rem(me + count - 1, count))
        stage_b[part, 0] = own(1, lax.rem(me + 1, count))
        for step in range(count - 1):
            slot = part * (count - 1) + step
            ahead = pltpu.make_async_remote_copy(
                src_ref=stage_f.at[part, step],
                dst_ref=land_f.at[part, step],
                send_sem=send_f.at[slot],
                recv_sem=recv_f.at[slot],
                device_id=(dom, right),
                device_id_type=mesh_ids,
            )
            behind = pltpu.make_async_remote_copy(
                src_ref=stage_b.at[part, step],
                dst_ref=land_b.at[part, step],
                send_sem=send_b.at[slot],
                recv_sem=recv_b.at[slot],
                device_id=(dom, left),
                device_id_type=mesh_ids,
            )
            ahead.start()
            behind.start()
            ahead.wait()
            behind.wait()
            forward_sum = land_f[part, step] + own(0, lax.rem(me + 2 * count - 2 - step, count))
            backward_sum = land_b[part, step] + own(1, lax.rem(me + 2 + step, count))
            if step < count - 2:
                stage_f[part, step + 1] = forward_sum
                stage_b[part, step + 1] = backward_sum
            else:
                o_ref[0, :, :, pl.ds(low, half)] = forward_sum
                o_ref[1, :, :, pl.ds(low, half)] = backward_sum


def exchange_and_sum(full):
    count = lax.axis_size("mat")
    domains = lax.axis_size("dom")
    slots, outputs, columns, rows, cols = full.shape
    share = rows // count
    half = cols // 2
    offsets = 2 * columns - 1
    piece = pltpu.VMEM((2, count - 1, offsets, share, half), jnp.float32)
    arrived = pltpu.VMEM((2, outputs, columns, rows, half), jnp.float32)
    return pl.pallas_call(
        functools.partial(exchange_kernel, count, domains, share, half),
        out_shape=jax.ShapeDtypeStruct((outputs, offsets, share, cols), jnp.float32),
        in_specs=[pl.BlockSpec(memory_space=pltpu.VMEM)],
        out_specs=pl.BlockSpec(memory_space=pltpu.VMEM),
        scratch_shapes=[
            pltpu.VMEM((2, outputs, offsets, rows, half), jnp.float32),
            arrived,
            arrived,
            piece,
            piece,
            piece,
            piece,
        ]
        + [pltpu.SemaphoreType.DMA((4,))] * 2
        + [pltpu.SemaphoreType.DMA((2 * (count - 1),))] * 4,
        compiler_params=pltpu.CompilerParams(
            collective_id=0, has_side_effects=True, vmem_limit_bytes=48 * 1024 * 1024
        ),
    )(full)


def on_device(orbitals, potential, centre_first, centre_second, centre_third, correlation_pairs):
    block_orbs, window_cells, second_cells, third_cells = orbitals.shape
    patch_cells = potential.shape[0]
    local_blocks = correlation_pairs.shape[0]
    per_block = block_orbs // local_blocks
    mat_count = lax.axis_size("mat")
    second_start = lax.axis_index("mat") * second_cells
    inside = sphere_mask(
        centre_first,
        centre_second,
        centre_third,
        window_cells,
        patch_cells,
        second_cells,
        second_start,
        second_cells * mat_count,
        third_cells,
    )
    masked = jnp.where(inside, orbitals, jnp.zeros_like(orbitals))
    upper_start = 2 * patch_cells
    to_right = masked[:, upper_start - 1 : window_cells - 1]
    to_left = masked[:, 1 : patch_cells + 1]
    from_left = passed_along(to_right, "dom", 1)
    from_right = passed_along(to_left, "dom", -1)
    mat_size = lax.axis_size("mat")
    up = [(i, (i + 1) % mat_size) for i in range(mat_size)]
    down = [(j, i) for i, j in up]
    row_above = lax.ppermute(masked[:, :, second_cells - 1], "mat", up)
    row_below = lax.ppermute(masked[:, :, 0], "mat", down)
    arrived = jnp.stack([from_left, from_right])
    arrived_above = lax.ppermute(arrived[:, :, :, second_cells - 1], "mat", up)
    arrived_below = lax.ppermute(arrived[:, :, :, 0], "mat", down)
    rows_from_left = jnp.stack([arrived_above[0], arrived_below[0]])
    rows_from_right = jnp.stack([arrived_above[1], arrived_below[1]])

    def with_rows(planes, rows):
        return jnp.concatenate([rows[0][:, :, None], planes, rows[1][:, :, None]], axis=2)

    zero_plane = jnp.zeros_like(masked[:, :1])
    zero_rows = jnp.zeros((2, block_orbs, 1, third_cells), masked.dtype)
    own_ext = with_rows(
        masked[:, patch_cells - 1 : upper_start + 1],
        jnp.stack([row_above[:, patch_cells - 1 : upper_start + 1], row_below[:, patch_cells - 1 : upper_start + 1]]),
    )
    left_ext = with_rows(
        jnp.concatenate([from_left, zero_plane, zero_plane], axis=1),
        jnp.concatenate([rows_from_left, zero_rows, zero_rows], axis=2),
    )
    right_ext = with_rows(
        jnp.concatenate([zero_plane, zero_plane, from_right], axis=1),
        jnp.concatenate([zero_rows, zero_rows, rows_from_right], axis=2),
    )
    phi_slots = [from_left[:, 1:], masked[:, patch_cells:upper_start], from_right[:, :-1]]
    plane_ranges = [(0, patch_cells - 1), (0, patch_cells), (1, patch_cells)]

    def overlap(a, b):
        low = max(plane_ranges[a][0], plane_ranges[b][0])
        high = min(plane_ranges[a][1], plane_ranges[b][1])
        first = phi_slots[a][:, low - plane_ranges[a][0] : high - plane_ranges[a][0]]
        second = phi_slots[b][:, low - plane_ranges[b][0] : high - plane_ranges[b][0]]
        return pair_product(first, second)

    def applied_overlap(a, b):
        low, high = plane_ranges[b]
        return pair_product(applied_slots[a][:, low:high], phi_slots[b])

    applied_slots = [
        stencil(ext, potential).astype(jnp.bfloat16) for ext in (left_ext, own_ext, right_ext)
    ]
    full = jnp.stack(
        [
            jnp.stack(
                [
                    jnp.stack([overlap(a, b) for a in range(3)]),
                    jnp.stack([applied_overlap(a, b) for a in range(3)]),
                ]
            )
            for b in range(3)
        ]
    )
    col_count = block_orbs // mat_count
    gram_rows, energy_rows = exchange_and_sum(full)
    columns = lax.axis_index("mat") * col_count + lax.iota(jnp.int32, col_count)
    block_ids = lax.iota(jnp.int32, local_blocks)
    column_pick = ((columns // per_block)[:, None] == block_ids[None, :]).astype(jnp.float32)
    row_pick = (
        (lax.iota(jnp.int32, block_orbs) // per_block)[:, None] == block_ids[None, :]
    ).astype(jnp.float32)
    select = jnp.einsum(
        "rkb,cb,ar->kca", correlation_pairs.astype(jnp.float32), column_pick, row_pick
    )
    return (gram_rows * select, energy_rows * select)


def solution(mesh):
    return jax.shard_map(
        on_device,
        mesh=mesh,
        in_specs=(
            P("dom", None, "mat", None),
            P("dom", "mat", None),
            P("dom"),
            P("dom"),
            P("dom"),
            P("dom", None, None),
        ),
        out_specs=(P(None, "mat", "dom"), P(None, "mat", "dom")),
        check_vma=False,
    )
```

```python
import jax
import jax.numpy as jnp
from jax import lax
from jax.sharding import PartitionSpec as P
from jax.experimental import pallas as pl
from jax.experimental.pallas import tpu as pltpu
import functools


def extended_2(array, sides, width):
    for axis, dim in sides:
        size, length = (lax.axis_size(axis), array.shape[dim])
        up = [(i, (i + 1) % size) for i in range(size)]
        down = [(j, i) for i, j in up]
        last = lax.slice_in_dim(array, length - width, length, axis=dim)
        first = lax.slice_in_dim(array, 0, width, axis=dim)
        before = lax.ppermute(last, axis, up)
        after = lax.ppermute(first, axis, down)
        array = jnp.concatenate([before, array, after], axis=dim)
    return array


def passed_along(block, axis, distance):
    devices = range(lax.axis_size(axis))
    route = [((i - distance) % len(devices), i) for i in devices]
    return lax.ppermute(block, axis, route)


def sphere_mask(
    centre_first,
    centre_second,
    centre_third,
    window_cells,
    patch_cells,
    second_cells,
    second_start,
    second_total,
    third_cells,
):
    planes = lax.iota(jnp.int32, window_cells)
    off_first = planes[None, :] - (patch_cells + centre_first[:, None])
    interior = (planes >= 1) & (planes <= window_cells - 2)
    second_coord = second_start + lax.iota(jnp.int32, second_cells)
    off_second = jnp.mod(second_coord[None, :] - centre_second[:, None], second_total)
    off_second = jnp.minimum(off_second, second_total - off_second)
    off_third = lax.iota(jnp.int32, third_cells)[None, :] - centre_third[:, None]
    radius = window_cells // 2
    distance = (
        (off_first * off_first)[:, :, None, None]
        + (off_second * off_second)[:, None, :, None]
        + (off_third * off_third)[:, None, None, :]
    )
    return (distance <= radius * radius) & interior[None, :, None, None]


def stencil(extended, potential_slab):
    centre_cells = extended[:, 1:-1, 1:-1, :].astype(jnp.float32)
    beside = extended[:, 2:, 1:-1, :].astype(jnp.float32) + extended[:, :-2, 1:-1, :].astype(
        jnp.float32
    )
    beside = (
        beside
        + extended[:, 1:-1, 2:, :].astype(jnp.float32)
        + extended[:, 1:-1, :-2, :].astype(jnp.float32)
    )
    third_padded = jnp.pad(centre_cells, ((0, 0), (0, 0), (0, 0), (1, 1)))
    beside = beside + third_padded[..., 2:] + third_padded[..., :-2]
    return 0.5 * (6.0 * centre_cells - beside) + potential_slab[None] * centre_cells


def pair_product(left, right):
    return lax.dot_general(
        left, right, (((1, 2, 3), (1, 2, 3)), ((), ())), preferred_element_type=jnp.float32
    )


def ring_scatter(full, axis):
    count = lax.axis_size("mat")
    me = lax.axis_index("mat")
    share = full.shape[axis] // count
    split = full.shape[-1] // 2
    halves = (full[..., :split], full[..., split:])
    forward = [(i, (i + 1) % count) for i in range(count)]
    backward = [((i + 1) % count, i) for i in range(count)]

    def chunk(values, index):
        return lax.dynamic_slice_in_dim(values, index * share, share, axis=axis)

    ahead = chunk(halves[0], lax.rem(me + count - 1, count))
    behind = chunk(halves[1], lax.rem(me + 1, count))
    for step in range(count - 1):
        ahead = lax.ppermute(ahead, "mat", forward)
        behind = lax.ppermute(behind, "mat", backward)
        ahead = ahead + chunk(halves[0], lax.rem(me + 2 * count - 2 - step, count))
        behind = behind + chunk(halves[1], lax.rem(me + 2 + step, count))
    return jnp.concatenate([ahead, behind], axis=-1)


def exchange_kernel(
    count, domains, share, half, x_ref, o_ref, total, from_left, from_right, stage_f, stage_b,
    land_f, land_b, dom_send, dom_recv, send_f, recv_f, send_b, recv_b,
):
    me = lax.axis_index("mat")
    dom = lax.axis_index("dom")
    right = lax.rem(me + 1, count)
    left = lax.rem(me + count - 1, count)
    up = lax.rem(dom + 1, domains)
    down = lax.rem(dom + domains - 1, domains)
    mesh_ids = pl.DeviceIdType.MESH
    barrier = pltpu.get_barrier_semaphore()
    for device in ((dom, left), (dom, right), (down, me), (up, me)):
        pl.semaphore_signal(barrier, 1, device_id=device, device_id_type=mesh_ids)
    pl.semaphore_wait(barrier, 4)

    exchanges = []
    for part in range(2):
        low = part * half
        to_down = pltpu.make_async_remote_copy(
            src_ref=x_ref.at[0, :, :, :, pl.ds(low, half)],
            dst_ref=from_right.at[part],
            send_sem=dom_send.at[2 * part],
            recv_sem=dom_recv.at[2 * part],
            device_id=(down, me),
            device_id_type=mesh_ids,
        )
        to_up = pltpu.make_async_remote_copy(
            src_ref=x_ref.at[2, :, :, :, pl.ds(low, half)],
            dst_ref=from_left.at[part],
            send_sem=dom_send.at[2 * part + 1],
            recv_sem=dom_recv.at[2 * part + 1],
            device_id=(up, me),
            device_id_type=mesh_ids,
        )
        to_down.start()
        to_up.start()
        exchanges.append((to_down, to_up))

    for part in range(2):
        low = part * half
        for copy in exchanges[part]:
            copy.wait()
        lefts, rights = from_left.at[part], from_right.at[part]
        here = total.at[part]
        here[:, 0] = lefts[:, 0]
        here[:, 1] = lefts[:, 1] + x_ref[1, :, 0, :, pl.ds(low, half)]
        here[:, 2] = lefts[:, 2] + x_ref[1, :, 1, :, pl.ds(low, half)] + rights[:, 0]
        here[:, 3] = x_ref[1, :, 2, :, pl.ds(low, half)] + rights[:, 1]
        here[:, 4] = rights[:, 2]

        def own(output, index):
            start = pl.multiple_of(index * share, share)
            return here[output, :, pl.ds(start, share), :]

        stage_f[part, 0] = own(0, lax.rem(me + count - 1, count))
        stage_b[part, 0] = own(1, lax.rem(me + 1, count))
        for step in range(count - 1):
            slot = part * (count - 1) + step
            ahead = pltpu.make_async_remote_copy(
                src_ref=stage_f.at[part, step],
                dst_ref=land_f.at[part, step],
                send_sem=send_f.at[slot],
                recv_sem=recv_f.at[slot],
                device_id=(dom, right),
                device_id_type=mesh_ids,
            )
            behind = pltpu.make_async_remote_copy(
                src_ref=stage_b.at[part, step],
                dst_ref=land_b.at[part, step],
                send_sem=send_b.at[slot],
                recv_sem=recv_b.at[slot],
                device_id=(dom, left),
                device_id_type=mesh_ids,
            )
            ahead.start()
            behind.start()
            ahead.wait()
            behind.wait()
            forward_sum = land_f[part, step] + own(0, lax.rem(me + 2 * count - 2 - step, count))
            backward_sum = land_b[part, step] + own(1, lax.rem(me + 2 + step, count))
            if step < count - 2:
                stage_f[part, step + 1] = forward_sum
                stage_b[part, step + 1] = backward_sum
            else:
                o_ref[0, :, :, pl.ds(low, half)] = forward_sum
                o_ref[1, :, :, pl.ds(low, half)] = backward_sum


def exchange_and_sum(full):
    count = lax.axis_size("mat")
    domains = lax.axis_size("dom")
    slots, outputs, columns, rows, cols = full.shape
    share = rows // count
    half = cols // 2
    offsets = 2 * columns - 1
    piece = pltpu.VMEM((2, count - 1, offsets, share, half), jnp.float32)
    arrived = pltpu.VMEM((2, outputs, columns, rows, half), jnp.float32)
    return pl.pallas_call(
        functools.partial(exchange_kernel, count, domains, share, half),
        out_shape=jax.ShapeDtypeStruct((outputs, offsets, share, cols), jnp.float32),
        in_specs=[pl.BlockSpec(memory_space=pltpu.VMEM)],
        out_specs=pl.BlockSpec(memory_space=pltpu.VMEM),
        scratch_shapes=[
            pltpu.VMEM((2, outputs, offsets, rows, half), jnp.float32),
            arrived,
            arrived,
            piece,
            piece,
            piece,
            piece,
        ]
        + [pltpu.SemaphoreType.DMA((4,))] * 2
        + [pltpu.SemaphoreType.DMA((2 * (count - 1),))] * 4,
        compiler_params=pltpu.CompilerParams(
            collective_id=0, has_side_effects=True, vmem_limit_bytes=48 * 1024 * 1024
        ),
    )(full)


def on_device(orbitals, potential, centre_first, centre_second, centre_third, correlation_pairs):
    block_orbs, window_cells, second_cells, third_cells = orbitals.shape
    patch_cells = potential.shape[0]
    local_blocks = correlation_pairs.shape[0]
    per_block = block_orbs // local_blocks
    mat_count = lax.axis_size("mat")
    second_start = lax.axis_index("mat") * second_cells
    inside = sphere_mask(
        centre_first,
        centre_second,
        centre_third,
        window_cells,
        patch_cells,
        second_cells,
        second_start,
        second_cells * mat_count,
        third_cells,
    )
    masked = jnp.where(inside, orbitals, jnp.zeros_like(orbitals))
    upper_start = 2 * patch_cells
    to_right = masked[:, upper_start - 1 : window_cells - 1]
    to_left = masked[:, 1 : patch_cells + 1]
    from_left = passed_along(to_right, "dom", 1)
    from_right = passed_along(to_left, "dom", -1)
    mat_size = lax.axis_size("mat")
    up = [(i, (i + 1) % mat_size) for i in range(mat_size)]
    down = [(j, i) for i, j in up]
    row_above = lax.ppermute(masked[:, :, second_cells - 1], "mat", up)
    row_below = lax.ppermute(masked[:, :, 0], "mat", down)
    arrived = jnp.stack([from_left, from_right])
    arrived_above = lax.ppermute(arrived[:, :, :, second_cells - 1], "mat", up)
    arrived_below = lax.ppermute(arrived[:, :, :, 0], "mat", down)
    rows_from_left = jnp.stack([arrived_above[0], arrived_below[0]])
    rows_from_right = jnp.stack([arrived_above[1], arrived_below[1]])

    def with_rows(planes, rows):
        return jnp.concatenate([rows[0][:, :, None], planes, rows[1][:, :, None]], axis=2)

    zero_plane = jnp.zeros_like(masked[:, :1])
    zero_rows = jnp.zeros((2, block_orbs, 1, third_cells), masked.dtype)
    own_ext = with_rows(
        masked[:, patch_cells - 1 : upper_start + 1],
        jnp.stack([row_above[:, patch_cells - 1 : upper_start + 1], row_below[:, patch_cells - 1 : upper_start + 1]]),
    )
    left_ext = with_rows(
        jnp.concatenate([from_left, zero_plane, zero_plane], axis=1),
        jnp.concatenate([rows_from_left, zero_rows, zero_rows], axis=2),
    )
    right_ext = with_rows(
        jnp.concatenate([zero_plane, zero_plane, from_right], axis=1),
        jnp.concatenate([zero_rows, zero_rows, rows_from_right], axis=2),
    )
    phi_slots = [
        jnp.concatenate([from_left[:, 1:], zero_plane], axis=1),
        masked[:, patch_cells:upper_start],
        jnp.concatenate([zero_plane, from_right[:, :-1]], axis=1),
    ]
    applied_slots = [
        stencil(ext, potential).astype(jnp.bfloat16) for ext in (left_ext, own_ext, right_ext)
    ]
    gram_blocks = {}

    def gram_block(a, b):
        if (b, a) in gram_blocks:
            return gram_blocks[(b, a)].T
        gram_blocks[(a, b)] = pair_product(phi_slots[a], phi_slots[b])
        return gram_blocks[(a, b)]

    full = jnp.stack(
        [
            jnp.stack(
                [
                    jnp.stack([gram_block(a, b) for a in range(3)]),
                    jnp.stack([pair_product(applied_slots[a], phi_slots[b]) for a in range(3)]),
                ]
            )
            for b in range(3)
        ]
    )
    col_count = block_orbs // mat_count
    gram_rows, energy_rows = exchange_and_sum(full)
    columns = lax.axis_index("mat") * col_count + lax.iota(jnp.int32, col_count)
    block_ids = lax.iota(jnp.int32, local_blocks)
    column_pick = ((columns // per_block)[:, None] == block_ids[None, :]).astype(jnp.float32)
    row_pick = (
        (lax.iota(jnp.int32, block_orbs) // per_block)[:, None] == block_ids[None, :]
    ).astype(jnp.float32)
    select = jnp.einsum(
        "rkb,cb,ar->kca", correlation_pairs.astype(jnp.float32), column_pick, row_pick
    )
    return (gram_rows * select, energy_rows * select)


def solution(mesh):
    return jax.shard_map(
        on_device,
        mesh=mesh,
        in_specs=(
            P("dom", None, "mat", None),
            P("dom", "mat", None),
            P("dom"),
            P("dom"),
            P("dom"),
            P("dom", None, None),
        ),
        out_specs=(P(None, "mat", "dom"), P(None, "mat", "dom")),
        check_vma=False,
    )
```
